32 devices in a mesh: dp: 16 (over z, y, x), mp: 2 (over core).
Axes of the slice: x: 2, y: 2, z: 4, core: 2. Of those that a mesh axis runs over, the one named last changes fastest.
Arguments:
- tokens: bfloat16 [24576, 768], P('dp'), may hold values from -6 to 6
- cotangent: bfloat16 [24576, 768], P('dp'), may hold values from -6 to 6
- device_class: int32 [16], P('dp'), may hold values from 0 to 2, as said below
- input_proj: float32 [768, 3, 768], P('dp', None, 'mp'), may hold values from -0.21875 to 0.21875
- output_proj: float32 [768, 768], P('dp', 'mp'), may hold values from -0.875 to 0.875
- expand_proj: float32 [768, 3072], P('dp', 'mp'), may hold values from -0.21875 to 0.21875
- reduce_proj: float32 [768, 3072], P('dp', 'mp'), may hold values from -0.109375 to 0.109375
- norm_params: float32 [768, 4], replicated, may hold values from -1.5 to 1.5, as said below
- rope_freqs: float32 [2, 12, 32], P(None, 'mp'), may hold values from -3 to 3
- input_first: float32 [768, 3, 768], P('dp', None, 'mp'), may hold values from -0.00061035156 to 0.00061035156
- input_second: float32 [768, 3, 768], P('dp', None, 'mp'), may hold values from 7.064254e-11 to 1.1302806e-09
- output_first: float32 [768, 768], P('dp', 'mp'), may hold values from -0.00061035156 to 0.00061035156
- output_second: float32 [768, 768], P('dp', 'mp'), may hold values from 7.064254e-11 to 1.1302806e-09
- expand_first: float32 [768, 3072], P('dp', 'mp'), may hold values from -0.00061035156 to 0.00061035156
- expand_second: float32 [768, 3072], P('dp', 'mp'), may hold values from 7.064254e-11 to 1.1302806e-09
- reduce_first: float32 [768, 3072], P('dp', 'mp'), may hold values from -0.00061035156 to 0.00061035156
- reduce_second: float32 [768, 3072], P('dp', 'mp'), may hold values from 7.064254e-11 to 1.1302806e-09
- norm_first: float32 [768, 4], replicated, may hold values from -0.0024414062 to 0.0024414062
- norm_second: float32 [768, 4], replicated, may hold values from 1.1302806e-09 to 1.808449e-08
- rope_first: float32 [2, 12, 32], P(None, 'mp'), may hold values from -0.005859375 to 0.005859375
- rope_second: float32 [2, 12, 32], P(None, 'mp'), may hold values from 7.064254e-09 to 1.13028065e-07
Outputs:
- activations: bfloat16 [24576, 768], P('dp')
- input_grad: float32 [24576, 768], P('dp')
- clip_norm: float32 [], replicated
- first_input: float32 [768, 3, 768], P('dp', None, 'mp')
- second_input: float32 [768, 3, 768], P('dp', None, 'mp')
- updated_input: float32 [768, 3, 768], P('dp', None, 'mp')
- first_output: float32 [768, 768], P('dp', 'mp')
- second_output: float32 [768, 768], P('dp', 'mp')
- updated_output: float32 [768, 768], P('dp', 'mp')
- first_expand: float32 [768, 3072], P('dp', 'mp')
- second_expand: float32 [768, 3072], P('dp', 'mp')
- updated_expand: float32 [768, 3072], P('dp', 'mp')
- first_reduce: float32 [768, 3072], P('dp', 'mp')
- second_reduce: float32 [768, 3072], P('dp', 'mp')
- updated_reduce: float32 [768, 3072], P('dp', 'mp')
- first_norm: float32 [768, 4], replicated
- second_norm: float32 [768, 4], replicated
- updated_norm: float32 [768, 4], replicated
- first_rope: float32 [2, 12, 32], P(None, 'mp')
- second_rope: float32 [2, 12, 32], P(None, 'mp')
- updated_rope: float32 [2, 12, 32], P(None, 'mp')
The draws below stay inside these ranges and needn't reach their ends.
Inputs may be any that keep to these rules, and one draw needn't show every extreme that they name: `device_class`: never falls along dp; each of the three classes holds at least one index of dp; the group sizes are drawn afresh. `norm_params`: columns 0 and 2 are gains, columns 1 and 3 shifts.
All inputs are finite; a program needn't handle non-finite values.
Results may differ from the reference program's by a relative error of at most 0.012.
Values may be sent and summed in bfloat16 or wider, within the bound.
No kernel may reach another device: no remote copies, remote signals or barrier semaphores. Data moves between devices by JAX's collectives and lax.ppermute only.
A program may use at most 192 MiB of HBM per device.

```python
import math
import jax
import jax.numpy as jnp
from jax import lax

D = 768
H = 12
HD = 64
MLP = 3072
SIDE_A = 14
SIDE_B = 20
SIDE_C = 24
STEP = 10
TOK_DEV = 1536
TOKENS = 24576
N_DP = 16


def draw_device_class(key, part):
    key_first, key_second = jax.random.split(key)
    first_cut = jax.random.randint(key_first, (), 1, N_DP - 1)
    second_cut = jax.random.randint(key_second, (), first_cut + 1, N_DP)
    places = jnp.arange(N_DP)
    return ((places >= first_cut).astype(jnp.int32) + (places >= second_cut).astype(jnp.int32)).astype(jnp.int32)


def draw_norm_params(key, part):
    key_gain, key_shift = jax.random.split(key)
    gains = jax.random.uniform(key_gain, (D, 2), jnp.float32, 0.5, 1.5)
    shifts = jnp.clip(0.3 * jax.random.normal(key_shift, (D, 2), jnp.float32), -1.5, 1.5)
    return jnp.stack([gains[:, 0], shifts[:, 0], gains[:, 1], shifts[:, 1]], axis=1)


def block_scale(rng, dims, shards, low, largest):
    factor_of, own = 1.0, jax.random.fold_in(rng, 6)
    for axis_at, blocks in shards:
        heights = jnp.exp(jax.random.uniform(jax.random.fold_in(own, axis_at), (blocks,), jnp.float32, low / len(shards), largest / len(shards)))
        factor_of = factor_of * jnp.repeat(heights, dims[axis_at] // blocks).reshape([-1 if axis == axis_at else 1 for axis in range(len(dims))])
    return factor_of


def bell_draw(rng, shape, scale, bound, shards=(), kind=jnp.bfloat16):
    values = jax.random.normal(rng, shape, jnp.float32) * scale
    if len(shards) > 0:
        values = block_scale(rng, shape, shards, -0.22, 0.18) * values
    return jnp.clip(values, min=-bound, max=bound).astype(kind)


def setup_inputs(seed: int = 0) -> dict:
    splits = jax.random.split(jax.random.key(seed), 22)
    return {
        "tokens": bell_draw(splits[0], (TOKENS, D), 1.0, 6.0, ((0, 16),)),
        "cotangent": bell_draw(splits[1], (TOKENS, D), 1.0, 6.0, ((0, 16),)),
        "device_class": draw_device_class(jax.random.fold_in(splits[21], 71), 0),
        "input_proj": bell_draw(splits[3], (D, 3, D), D ** -0.5, 0.21875, ((0, 16), (2, 2)), jnp.float32),
        "output_proj": bell_draw(splits[4], (D, D), (D // 16) ** -0.5, 0.875, ((0, 16), (1, 2)), jnp.float32),
        "expand_proj": bell_draw(splits[5], (D, MLP), D ** -0.5, 0.21875, ((0, 16), (1, 2)), jnp.float32),
        "reduce_proj": bell_draw(splits[6], (D, MLP), MLP ** -0.5, 0.109375, ((0, 16), (1, 2)), jnp.float32),
        "norm_params": draw_norm_params(jax.random.fold_in(splits[21], 71), 0),
        "rope_freqs": bell_draw(splits[8], (2, H, HD // 2), 0.3, 3.0, ((1, 2),), jnp.float32),
        "input_first": bell_draw(splits[9], (D, 3, D), (0.11 / (4 * D * D + 2 * D * MLP) ** 0.5), 0.00061035156, ((0, 16), (2, 2)), jnp.float32),
        "input_second": jnp.clip(jnp.exp(math.log(1.130280646854942e-09) - 2.7725887 * jax.random.uniform(splits[10], (D, 3, D), jnp.float32) ** block_scale(splits[10], (D, 3, D), ((0, 16), (2, 2)), -0.2, 0.2)), 7.064254042843388e-11, 1.130280646854942e-09),
        "output_first": bell_draw(splits[11], (D, D), (0.11 / (4 * D * D + 2 * D * MLP) ** 0.5), 0.00061035156, ((0, 16), (1, 2)), jnp.float32),
        "output_second": jnp.clip(jnp.exp(math.log(1.130280646854942e-09) - 2.7725887 * jax.random.uniform(splits[12], (D, D), jnp.float32) ** block_scale(splits[12], (D, D), ((0, 16), (1, 2)), -0.2, 0.2)), 7.064254042843388e-11, 1.130280646854942e-09),
        "expand_first": bell_draw(splits[13], (D, MLP), (0.11 / (4 * D * D + 2 * D * MLP) ** 0.5), 0.00061035156, ((0, 16), (1, 2)), jnp.float32),
        "expand_second": jnp.clip(jnp.exp(math.log(1.130280646854942e-09) - 2.7725887 * jax.random.uniform(splits[14], (D, MLP), jnp.float32) ** block_scale(splits[14], (D, MLP), ((0, 16), (1, 2)), -0.2, 0.2)), 7.064254042843388e-11, 1.130280646854942e-09),
        "reduce_first": bell_draw(splits[15], (D, MLP), (0.11 / (4 * D * D + 2 * D * MLP) ** 0.5), 0.00061035156, ((0, 16), (1, 2)), jnp.float32),
        "reduce_second": jnp.clip(jnp.exp(math.log(1.130280646854942e-09) - 2.7725887 * jax.random.uniform(splits[16], (D, MLP), jnp.float32) ** block_scale(splits[16], (D, MLP), ((0, 16), (1, 2)), -0.2, 0.2)), 7.064254042843388e-11, 1.130280646854942e-09),
        "norm_first": bell_draw(splits[17], (D, 4), (0.44 / (4 * D * D + 2 * D * MLP) ** 0.5), 0.0024414062, (), jnp.float32),
        "norm_second": jnp.clip(jnp.exp(jax.random.uniform(splits[18], (D, 4), jnp.float32, math.log(1.130280646854942e-09), math.log(1.8084490349679072e-08))), 1.130280646854942e-09, 1.8084490349679072e-08),
        "rope_first": bell_draw(splits[19], (2, H, HD // 2), (1.1 / (4 * D * D + 2 * D * MLP) ** 0.5), 0.005859375, ((1, 2),), jnp.float32),
        "rope_second": jnp.clip(jnp.exp(math.log(1.1302806512958341e-07) - 2.7725887 * jax.random.uniform(splits[20], (2, H, HD // 2), jnp.float32) ** block_scale(splits[20], (2, H, HD // 2), ((1, 2),), -0.2, 0.2)), 7.064254070598963e-09, 1.1302806512958341e-07),
    }


highest = lax.Precision.HIGHEST
norm_epsilon = 1e-06
adam_epsilon = 1e-08
beta_first = 0.9
beta_second = 0.999
clip_limit = 1.0
matrix_rate = 0.05
matrix_decay = 0.05
vector_rate = 0.5

@jax.custom_vjp
def low(v):
    return lax.optimization_barrier(v.astype(jnp.bfloat16)).astype(jnp.float32)

@jax.custom_vjp
def low_back(v):
    return v

def low_keep(v):
    return (low(v), None)

def low_pass(kept, grad):
    return (grad,)

def back_keep(v):
    return (v, None)

def back_low(kept, grad):
    return (low(grad),)
low.defvjp(low_keep, low_pass)
low_back.defvjp(back_keep, back_low)

def layer_norm(values, gain_vec, shift_vec):
    center = values - lax.optimization_barrier(jnp.mean(values, axis=-1, keepdims=True))
    spread = lax.optimization_barrier(jnp.mean(center * center, axis=-1, keepdims=True))
    return center * lax.rsqrt(spread + norm_epsilon) * gain_vec + shift_vec

def slab_layout(resolution):
    places = jnp.arange(TOK_DEV, dtype=jnp.int32)
    side_len = jnp.where(resolution == 0, SIDE_A, jnp.where(resolution == 1, SIDE_B, SIDE_C)).astype(jnp.int32)
    patches = side_len * side_len
    image_id = places // patches
    within = places % patches
    column = (within % side_len).astype(jnp.float32)
    row_pos = (within // side_len).astype(jnp.float32)
    usable = (image_id < TOK_DEV // patches).astype(jnp.float32)
    return (image_id, column, row_pos, usable)

def rotate(values, cosine, sine):
    halfway = values.shape[-1] // 2
    former = values[..., :halfway]
    latter = values[..., halfway:]
    return jnp.concatenate([former * cosine - latter * sine, former * sine + latter * cosine], axis=-1)

def slab_layer(params, inputs, resolution):
    input_proj, output_proj, expand_proj, reduce_proj, norm_params, rope_freqs = params
    image_id, column, row_pos, usable = slab_layout(resolution)
    normed = low(layer_norm(inputs, norm_params[:, 0], norm_params[:, 1]))
    joined = low_back(jnp.einsum('td,dke->tke', normed, low(input_proj), precision=highest))
    joined = joined.reshape(TOK_DEV, 3, H, HD)
    angles = column[:, None, None] * rope_freqs[0][None] + row_pos[:, None, None] * rope_freqs[1][None]
    cosine = jnp.cos(angles)
    sine = jnp.sin(angles)
    queries = low(rotate(joined[:, 0], cosine, sine))
    keys_rot = low(rotate(joined[:, 1], cosine, sine))
    values_in = low(joined[:, 2])
    row_block = min(512, TOK_DEV)
    blocks = TOK_DEV // row_block

    def attend(pair):
        query_block, block_ids = pair
        scores = low_back(jnp.einsum('qhe,khe->hqk', query_block, keys_rot, precision=highest) * 0.125)
        same = (block_ids[:, None] == image_id[None, :])[None]
        scores = jnp.where(same, scores, -1e+30)
        probs = low(jax.nn.softmax(scores, axis=-1))
        return jnp.einsum('hqk,khe->qhe', probs, values_in, precision=highest)
    mixed = lax.map(jax.checkpoint(attend), (queries.reshape(blocks, row_block, H, HD), image_id.reshape(blocks, row_block)))
    mixed = low(low_back(mixed.reshape(TOK_DEV, D)))
    attn_out = low_back(jnp.dot(mixed, low(output_proj).T, precision=highest))
    hidden = inputs + attn_out
    second_in = low(layer_norm(hidden, norm_params[:, 2], norm_params[:, 3]))
    expanded = low_back(jnp.dot(second_in, low(expand_proj), precision=highest))
    activ = low(jax.nn.gelu(expanded, approximate=False))
    mlp_out = low_back(jnp.dot(activ, low(reduce_proj).T, precision=highest))
    return hidden + mlp_out

def adamw(weight, first, second, gradient, rate, decay):
    first = beta_first * first + (1.0 - beta_first) * gradient
    second = beta_second * second + (1.0 - beta_second) * gradient * gradient
    first_fix = 1.0 - beta_first ** STEP
    second_fix = 1.0 - beta_second ** STEP
    update = first / first_fix / (jnp.sqrt(second / second_fix) + adam_epsilon)
    return (first, second, weight - rate * (update + decay * weight))

def reference(tokens, cotangent, device_class, input_proj, output_proj, expand_proj, reduce_proj, norm_params, rope_freqs, input_first, input_second, output_first, output_second, expand_first, expand_second, reduce_first, reduce_second, norm_first, norm_second, rope_first, rope_second):
    params = (input_proj, output_proj, expand_proj, reduce_proj, norm_params, rope_freqs)
    slabs = tokens.astype(jnp.float32).reshape(N_DP, TOK_DEV, D)

    def forward(weights, inputs):

        def one_slab(pair):
            return jax.checkpoint(slab_layer)(weights, pair[0], pair[1])
        return lax.map(one_slab, (inputs, device_class))
    outputs, pullback = jax.vjp(forward, params, slabs)
    usable = jax.vmap(lambda resolution: slab_layout(resolution)[3])(device_class)
    upstream = cotangent.astype(jnp.float32).reshape(N_DP, TOK_DEV, D) * usable[:, :, None]
    grads, slab_grads = pullback(upstream)
    total = jnp.zeros((), jnp.float32)
    for gradient in grads:
        total = total + jnp.sum(gradient * gradient)
    clip_norm = jnp.sqrt(total)
    factor = jnp.minimum(1.0, clip_limit / clip_norm)
    first_input, second_input, updated_input = adamw(input_proj, input_first, input_second, grads[0] * factor, matrix_rate, matrix_decay)
    first_output, second_output, updated_output = adamw(output_proj, output_first, output_second, grads[1] * factor, matrix_rate, matrix_decay)
    first_expand, second_expand, updated_expand = adamw(expand_proj, expand_first, expand_second, grads[2] * factor, matrix_rate, matrix_decay)
    first_reduce, second_reduce, updated_reduce = adamw(reduce_proj, reduce_first, reduce_second, grads[3] * factor, matrix_rate, matrix_decay)
    first_norm, second_norm, updated_norm = adamw(norm_params, norm_first, norm_second, grads[4] * factor, vector_rate, 0.0)
    first_rope, second_rope, updated_rope = adamw(rope_freqs, rope_first, rope_second, grads[5] * factor, vector_rate, 0.0)
    activations = outputs.reshape(TOKENS, D).astype(jnp.bfloat16)
    input_grad = slab_grads.reshape(TOKENS, D)
    return (activations, input_grad, clip_norm, first_input, second_input, updated_input, first_output, second_output, updated_output, first_expand, second_expand, updated_expand, first_reduce, second_reduce, updated_reduce, first_norm, second_norm, updated_norm, first_rope, second_rope, updated_rope)
```

```python
from functools import partial

import jax
import jax.numpy as jnp
from jax import lax
from jax.experimental import pallas as pl
from jax.experimental.pallas import tpu as pltpu
from jax.sharding import PartitionSpec as P

HD = 64
SIDES = (14, 20, 24)
STEP = 10
TOK_DEV = 1536

norm_epsilon = 1e-06
adam_epsilon = 1e-08
beta_first = 0.9
beta_second = 0.999
clip_limit = 1.0
matrix_rate = 0.05
matrix_decay = 0.05
vector_rate = 0.5

bf16 = jnp.bfloat16
f32 = jnp.float32
NT = (((1,), (1,)), ((), ()))
NN = (((1,), (0,)), ((), ()))
TN = (((0,), (0,)), ((), ()))
LANES = 128
MIB = 1024 * 1024


def dot(a, b, dims):
    return lax.dot_general(a, b, dims, preferred_element_type=f32)


def swap(value, axis, size, bit):
    return lax.ppermute(value, axis, [(i, i ^ bit) for i in range(size)])


def bits_of(size):
    return [1 << b for b in reversed(range(size.bit_length() - 1))]


def orders(size):
    bits = bits_of(size)
    return (bits, bits[:-2] + [bits[-1], bits[-2]])


def masks_of(order):
    masks = [0]
    for bit in order:
        masks = masks + [m ^ bit for m in masks]
    return masks


def gather(shard, size):
    cur = shard[None]
    for bit in bits_of(size)[:-2]:
        cur = jnp.concatenate([cur, swap(cur, "dp", size, bit)], axis=0)
    half = shard.shape[1] // 2
    out = []
    for color, order in enumerate(orders(size)):
        part = cur[:, :, color * half : (color + 1) * half]
        part = jnp.concatenate([part, swap(part, "dp", size, order[-2])], axis=0)
        out.append((part, swap(part, "dp", size, order[-1])))
    return out


def whole(pieces, size, me):
    rows, half = pieces[0][0].shape[1:]
    masks = [masks_of(order) for order in orders(size)]
    if rows % 16:
        cols = []
        for (low, high), ms in zip(pieces, masks):
            place = [0] * size
            for at, m in enumerate(ms):
                place[m] = at
            both = jnp.concatenate([low, high], axis=0)
            index = jnp.array(place, jnp.int32)[jnp.arange(size, dtype=jnp.int32) ^ me]
            cols.append(jnp.take(both, index, axis=0).reshape(size * rows, half))
        return jnp.concatenate(cols, axis=1)

    def kernel(me_ref, a0, a1, b0, b1, out):
        own = me_ref[0]
        for color, pair in enumerate(((a0, a1), (b0, b1))):
            for j, mask in enumerate(masks[color]):
                src = pair[j // (size // 2)]
                at = pl.multiple_of((own ^ mask) * rows, 16)
                out[pl.ds(at, rows), color * half : (color + 1) * half] = src[j % (size // 2)]

    flat = [p for pair in pieces for p in pair]
    return pl.pallas_call(
        kernel,
        out_shape=jax.ShapeDtypeStruct((size * rows, 2 * half), bf16),
        grid_spec=pltpu.PrefetchScalarGridSpec(
            num_scalar_prefetch=1,
            grid=(1,),
            in_specs=[pl.BlockSpec(p.shape, lambda i, c: (0, 0, 0)) for p in flat],
            out_specs=pl.BlockSpec((size * rows, 2 * half), lambda i, c: (0, 0)),
        ),
        compiler_params=pltpu.CompilerParams(vmem_limit_bytes=24 * MIB),
        name="whole",
    )(me[None], *flat)


def grad_halves(terms, order, size, me):
    ms = masks_of(order)
    count = size // 2
    feats = terms[0][0].shape[1]
    rows = feats // size
    width = sum(w for _, _, _, w in terms)
    if rows % 16:
        mat = jnp.concatenate(
            [dot(l, r[:, c * w : (c + 1) * w], TN) for l, r, c, w in terms], axis=1
        ).reshape(size, rows, width)
        mat = jnp.take(mat, jnp.array(ms, jnp.int32) ^ me, axis=0)
        return mat[:count], mat[count:].astype(bf16)

    def kernel(me_ref, *refs):
        ins, (keep, send, acc) = refs[: 2 * len(terms)], refs[2 * len(terms) :]
        own = me_ref[0]
        at = 0
        for t, (_, _, _, w) in enumerate(terms):
            acc[:, at : at + w] = dot(ins[2 * t][...], ins[2 * t + 1][...], TN)
            at += w
        for j, mask in enumerate(ms):
            block = acc[pl.ds(pl.multiple_of((own ^ mask) * rows, 16), rows), :]
            if j < count:
                keep[j] = block
            else:
                send[j - count] = block.astype(bf16)

    in_specs, args = [], []
    for l, r, c, w in terms:
        in_specs.append(pl.BlockSpec(l.shape, lambda i, m: (0, 0)))
        in_specs.append(pl.BlockSpec((r.shape[0], w), lambda i, m, c=c: (0, c)))
        args += [l, r]
    flops = sum(2 * l.shape[0] * l.shape[1] * w for l, _, _, w in terms)
    return pl.pallas_call(
        kernel,
        out_shape=(
            jax.ShapeDtypeStruct((count, rows, width), f32),
            jax.ShapeDtypeStruct((count, rows, width), bf16),
        ),
        grid_spec=pltpu.PrefetchScalarGridSpec(
            num_scalar_prefetch=1,
            grid=(1,),
            in_specs=in_specs,
            out_specs=[pl.BlockSpec((count, rows, width), lambda i, m: (0, 0, 0))] * 2,
            scratch_shapes=[pltpu.VMEM((feats, width), f32)],
        ),
        compiler_params=pltpu.CompilerParams(vmem_limit_bytes=40 * MIB),
        cost_estimate=pl.CostEstimate(flops=flops, transcendentals=0, bytes_accessed=12 * MIB),
        name="grad_halves",
    )(me[None], *args)


def scatter(halves, size):
    parts = []
    for order, (keep, send) in zip(orders(size), halves):
        total = keep + swap(send, "dp", size, order[-1]).astype(f32)
        count = total.shape[0] // 2
        parts.append(
            total[:count] + swap(total[count:].astype(bf16), "dp", size, order[-2]).astype(f32)
        )
    total = jnp.concatenate(parts, axis=2)
    for bit in bits_of(size)[:-2][::-1]:
        count = total.shape[0] // 2
        total = total[:count] + swap(total[count:].astype(bf16), "dp", size, bit).astype(f32)
    return total[0]


def pair_sum(part):
    return part.astype(f32) + lax.ppermute(part, "mp", [(0, 1), (1, 0)]).astype(f32)


def butterfly(value, size):
    for bit in bits_of(size)[::-1]:
        value = value + swap(value, "dp", size, bit)
    return value


def images(level, visit_dynamic, visit):
    side = SIDES[level]
    patches = side * side
    count = -(-TOK_DEV // patches)
    if patches % 16 == 0:
        for i in range(count):
            visit(i * patches, min(patches, TOK_DEV - i * patches))
        return
    window = -(-(patches + 12) // 16) * 16

    def one(i, carry):
        first = i * patches
        at = pl.multiple_of(jnp.minimum(first // 16 * 16, TOK_DEV - window), 16)
        visit_dynamic(at, window, first - at, jnp.minimum(first + patches, TOK_DEV) - at)
        return carry

    lax.fori_loop(0, count, one, 0)


def heads_of(block):
    lane = lax.broadcasted_iota(jnp.int32, block.shape, 1)
    zero = jnp.zeros_like(block)
    return jnp.where(lane < HD, block, zero), jnp.where(lane < HD, zero, block)


def blocks_of(window):
    for size in (192, 208, 200, 176, 336, 400):
        if window % size == 0 and size % 16 == 0:
            return size
    return window


def attend_kernel(level_ref, q_ref, k_ref, v_ref, o_ref):
    def softmax_mix(queries, keys, values, lo=None, hi=None):
        mixes = []
        for head in heads_of(queries):
            scores = dot(head, keys, NT)
            if lo is not None:
                place = lax.broadcasted_iota(jnp.int32, scores.shape, 1)
                scores = jnp.where((place >= lo) & (place < hi), scores, -1e30)
            expo = jnp.exp(scores - jnp.max(scores, axis=-1, keepdims=True))
            total = jnp.sum(expo, axis=-1, keepdims=True)
            mixes.append(dot(expo.astype(bf16), values, NN) / total)
        lane = lax.broadcasted_iota(jnp.int32, mixes[0].shape, 1)
        return jnp.where(lane < HD, mixes[0], mixes[1])

    def visit(at, window):
        keys, values = k_ref[pl.ds(at, window), :], v_ref[pl.ds(at, window), :]
        size = blocks_of(window)

        def block(b, carry):
            rows = pl.ds(pl.multiple_of(at + b * size, 16), size)
            o_ref[rows, :] = softmax_mix(q_ref[rows, :], keys, values).astype(bf16)
            return carry

        lax.fori_loop(0, window // size, block, 0)

    def visit_dynamic(at, window, lo, hi):
        rows = pl.ds(at, window)
        mix = softmax_mix(q_ref[rows, :], k_ref[rows, :], v_ref[rows, :], lo, hi)
        place = lax.broadcasted_iota(jnp.int32, mix.shape, 0)
        own = (place >= lo) & (place < hi)
        o_ref[rows, :] = jnp.where(own, mix, o_ref[rows, :].astype(f32)).astype(bf16)

    for level in range(3):

        @pl.when(level_ref[0] == level)
        def _(level=level):
            images(level, visit_dynamic, visit)


def attend(level, qkv, pairs):
    tokens = qkv.shape[0]
    spec = lambda which: pl.BlockSpec((tokens, LANES), lambda p, c: (0, which * pairs + p))
    return pl.pallas_call(
        attend_kernel,
        out_shape=jax.ShapeDtypeStruct((tokens, pairs * LANES), bf16),
        grid_spec=pltpu.PrefetchScalarGridSpec(
            num_scalar_prefetch=1,
            grid=(pairs,),
            in_specs=[spec(0), spec(1), spec(2)],
            out_specs=spec(0),
        ),
        compiler_params=pltpu.CompilerParams(vmem_limit_bytes=24 * MIB),
        cost_estimate=pl.CostEstimate(flops=8_000_000_000, transcendentals=5_000_000, bytes_accessed=5 * MIB),
        name="attend",
    )(level, qkv, qkv, qkv)


def partner(values):
    lane = lax.broadcasted_iota(jnp.int32, values.shape, values.ndim - 1)
    half = HD // 2
    width = values.shape[-1]
    return jnp.where(
        lane % HD < half,
        pltpu.roll(values, width - half, values.ndim - 1),
        pltpu.roll(values, half, values.ndim - 1),
    )


def attend_back_kernel(
    level_ref, q_ref, k_ref, v_ref, do_ref, cos_ref, sin_ref, col_ref, row_ref,
    dq_ref, dk_ref, dv_ref, freq_ref, dq_acc, dk_acc, dv_acc,
):
    def grads(at_q, size, at, window, lo=None, hi=None):
        rows, cols = pl.ds(at_q, size), pl.ds(at, window)
        keys, values = k_ref[cols, :], v_ref[cols, :]
        dq = jnp.zeros((size, LANES), f32)
        dk = jnp.zeros((window, LANES), f32)
        dv = jnp.zeros((window, LANES), f32)
        for query, grad, key in zip(heads_of(q_ref[rows, :]), heads_of(do_ref[rows, :]), heads_of(keys)):
            scores = dot(keys, query, NT)
            if lo is not None:
                place = lax.broadcasted_iota(jnp.int32, scores.shape, 0)
                scores = jnp.where((place >= lo) & (place < hi), scores, -1e30)
            expo = jnp.exp(scores - jnp.max(scores, axis=0, keepdims=True))
            probs = expo * (1.0 / jnp.sum(expo, axis=0, keepdims=True))
            if lo is not None:
                asked = lax.broadcasted_iota(jnp.int32, scores.shape, 1)
                probs = jnp.where((asked >= lo) & (asked < hi), probs, 0.0)
            dv = dv + dot(probs.astype(bf16), grad, NN)
            prob_grad = dot(values, grad, NT)
            inner = jnp.sum(probs * prob_grad, axis=0, keepdims=True)
            score_low = (probs * (prob_grad - inner)).astype(bf16)
            dk = dk + dot(score_low, query, NN)
            dq = dq + dot(score_low, key, TN)
        dq_acc[rows, :] += dq
        dk_acc[cols, :] += dk
        dv_acc[cols, :] += dv

    def visit(at, window):
        size = blocks_of(window)

        def block(b, carry):
            grads(pl.multiple_of(at + b * size, 16), size, at, window)
            return carry

        lax.fori_loop(0, window // size, block, 0)

    def visit_dynamic(at, window, lo, hi):
        grads(at, window, at, window, lo, hi)

    dq_acc[...] = jnp.zeros_like(dq_acc)
    dk_acc[...] = jnp.zeros_like(dk_acc)
    dv_acc[...] = jnp.zeros_like(dv_acc)
    for level in range(3):

        @pl.when(level_ref[0] == level)
        def _(level=level):
            images(level, visit_dynamic, visit)

    cosine, sine = cos_ref[...], sin_ref[...]
    dq, dk = dq_acc[...] * 0.125, dk_acc[...]
    dq_other, dk_other = partner(dq), partner(dk)
    dq_ref[...] = (dq * cosine - dq_other * sine).astype(bf16)
    dk_ref[...] = (dk * cosine - dk_other * sine).astype(bf16)
    dv_ref[...] = dv_acc[...].astype(bf16)
    turn = q_ref[...].astype(f32) * 8.0 * dq_other + k_ref[...].astype(f32) * dk_other
    freq_ref[0, 0:1, :] = jnp.sum(col_ref[...] * turn, axis=0, keepdims=True)
    freq_ref[0, 1:2, :] = jnp.sum(row_ref[...] * turn, axis=0, keepdims=True)


def attend_back(level, qkv, mixed_grad, cosine, sine, column, row_pos, pairs):
    tokens = qkv.shape[0]
    spec = lambda which: pl.BlockSpec((tokens, LANES), lambda p, c: (0, which * pairs + p))
    fixed = pl.BlockSpec((tokens, LANES), lambda p, c: (0, 0))
    out = jax.ShapeDtypeStruct((tokens, pairs * LANES), bf16)
    return pl.pallas_call(
        attend_back_kernel,
        out_shape=(out, out, out, jax.ShapeDtypeStruct((pairs, 2, LANES), f32)),
        grid_spec=pltpu.PrefetchScalarGridSpec(
            num_scalar_prefetch=1,
            grid=(pairs,),
            in_specs=[spec(0), spec(1), spec(2), spec(0), spec(0), spec(0), fixed, fixed],
            out_specs=[spec(0), spec(0), spec(0), pl.BlockSpec((1, 2, LANES), lambda p, c: (p, 0, 0))],
            scratch_shapes=[pltpu.VMEM((tokens, LANES), f32)] * 3,
        ),
        compiler_params=pltpu.CompilerParams(vmem_limit_bytes=40 * MIB),
        cost_estimate=pl.CostEstimate(flops=25_000_000_000, transcendentals=5_000_000, bytes_accessed=12 * MIB),
        name="attend_back",
    )(level, qkv, qkv, qkv, mixed_grad, cosine, sine, column, row_pos)


def slab_layout(resolution):
    places = jnp.arange(TOK_DEV, dtype=jnp.int32)
    side_len = jnp.where(
        resolution == 0, SIDES[0], jnp.where(resolution == 1, SIDES[1], SIDES[2])
    ).astype(jnp.int32)
    patches = side_len * side_len
    image_id = places // patches
    within = places % patches
    column = (within % side_len).astype(f32)
    row_pos = (within // side_len).astype(f32)
    usable = (image_id < TOK_DEV // patches).astype(f32)
    return (column, row_pos, usable)


def norm_forward(values, gain_vec, shift_vec):
    center = values - jnp.mean(values, axis=-1, keepdims=True)
    spread = jnp.mean(center * center, axis=-1, keepdims=True)
    scale_rows = lax.rsqrt(spread + norm_epsilon)
    unit_rows = center * scale_rows
    return (unit_rows * gain_vec + shift_vec, unit_rows, scale_rows)


def norm_backward(grad_rows, unit_rows, scale_rows, gain_vec):
    gain_grad = jnp.sum(grad_rows * unit_rows, axis=0)
    shift_grad = jnp.sum(grad_rows, axis=0)
    scaled = grad_rows * gain_vec
    values_grad = scale_rows * (
        scaled
        - jnp.mean(scaled, axis=-1, keepdims=True)
        - unit_rows * jnp.mean(scaled * unit_rows, axis=-1, keepdims=True)
    )
    return (values_grad, gain_grad, shift_grad)


def adamw(weight, first, second, gradient, rate, decay):
    first = beta_first * first + (1.0 - beta_first) * gradient
    second = beta_second * second + (1.0 - beta_second) * gradient * gradient
    first_fix = 1.0 - beta_first**STEP
    second_fix = 1.0 - beta_second**STEP
    update = first / first_fix / (jnp.sqrt(second / second_fix) + adam_epsilon)
    return (first, second, weight - rate * (update + decay * weight))


def local(
    size,
    tokens,
    cotangent,
    device_class,
    input_proj,
    output_proj,
    expand_proj,
    reduce_proj,
    norm_params,
    rope_freqs,
    input_first,
    input_second,
    output_first,
    output_second,
    expand_first,
    expand_second,
    reduce_first,
    reduce_second,
    norm_first,
    norm_second,
    rope_first,
    rope_second,
):
    heads = rope_freqs.shape[1]
    width = heads * HD
    pairs = width // LANES
    me = lax.axis_index("dp").astype(jnp.int32)
    lead_data = (me == 0).astype(f32)
    lead_model = (lax.axis_index("mp") == 0).astype(f32)
    rows = input_proj.shape[0]

    attn_shard = jnp.concatenate(
        [input_proj.reshape(rows, 3 * width).astype(bf16), output_proj.astype(bf16)], axis=1
    )
    attn_pieces = gather(attn_shard, size)
    expand_pieces = gather(expand_proj.astype(bf16), size)
    reduce_pieces = gather(reduce_proj.astype(bf16), size)

    column, row_pos, usable = slab_layout(device_class[0])
    inputs = tokens.astype(f32)
    normed_full, unit_one, scale_one = norm_forward(inputs, norm_params[:, 0], norm_params[:, 1])
    normed = normed_full.astype(bf16)
    freqs = jnp.concatenate([rope_freqs, rope_freqs], axis=2).reshape(2, width)
    angles = column[:, None] * freqs[0][None] + row_pos[:, None] * freqs[1][None]
    cosine = jnp.cos(angles)
    half = HD // 2
    sign = jnp.where(jnp.arange(width) % HD < half, -1.0, 1.0)
    sine = jnp.sin(angles) * sign[None]
    column = jnp.broadcast_to(column[:, None], (TOK_DEV, LANES))
    row_pos = jnp.broadcast_to(row_pos[:, None], (TOK_DEV, LANES))

    attn_whole = whole(attn_pieces, size, me)
    whole_in = attn_whole[:, : 3 * width]
    whole_out = attn_whole[:, 3 * width :]
    joined = dot(normed, whole_in, NN)

    def turned(values):
        heads_in = values.reshape(TOK_DEV, heads, 2, half)
        other = jnp.concatenate([heads_in[:, :, 1:], heads_in[:, :, :1]], axis=2).reshape(TOK_DEV, width)
        return values * cosine + other * sine

    qkv = jnp.concatenate(
        [
            (turned(joined[:, :width]) * 0.125).astype(bf16),
            turned(joined[:, width : 2 * width]).astype(bf16),
            joined[:, 2 * width :].astype(bf16),
        ],
        axis=1,
    )
    mixed = attend(device_class, qkv, pairs)
    hidden_rows = inputs + pair_sum(dot(mixed, whole_out, NT).astype(bf16))
    second_full, unit_two, scale_two = norm_forward(hidden_rows, norm_params[:, 2], norm_params[:, 3])
    second_in = second_full.astype(bf16)
    whole_expand = whole(expand_pieces, size, me)
    whole_reduce = whole(reduce_pieces, size, me)
    expanded = dot(second_in, whole_expand, NN)
    below = 0.5 * (1.0 + lax.erf(expanded * (0.5**0.5)))
    activ = (expanded * below).astype(bf16)
    slope = below + expanded * jnp.exp(-0.5 * expanded * expanded) * 0.3989422804014327
    upstream = cotangent.astype(f32) * usable[:, None]
    upstream_low = upstream.astype(bf16)
    hidden_low = dot(upstream_low, whole_reduce, NN)
    expanded_low = (hidden_low * slope).astype(bf16)
    wide = activ.shape[1] // 2
    reduce_shard = scatter(
        [
            grad_halves([(upstream_low, activ, c, wide)], order, size, me)
            for c, order in enumerate(orders(size))
        ],
        size,
    )
    second_part = dot(expanded_low, whole_expand, NT).astype(bf16)
    second_grad = pair_sum(second_part)
    expand_shard = scatter(
        [
            grad_halves([(second_in, expanded_low, c, wide)], order, size, me)
            for c, order in enumerate(orders(size))
        ],
        size,
    )
    activations = (hidden_rows + pair_sum(dot(activ, whole_reduce, NT).astype(bf16))).astype(bf16)
    hidden_norm_grad, gain_two, shift_two = norm_backward(second_grad, unit_two, scale_two, norm_params[:, 2])
    hidden_grad = upstream + hidden_norm_grad
    attn_low = hidden_grad.astype(bf16)
    mixed_low = dot(attn_low, whole_out, NN).astype(bf16)
    dq, dk, dv, turn = attend_back(
        device_class, qkv, mixed_low, cosine, sine, column, row_pos, pairs
    )
    freq_grad = turn.transpose(1, 0, 2).reshape(2, heads, HD)
    freq_grad = freq_grad[:, :, :half] - freq_grad[:, :, half:]
    joined_grad = jnp.concatenate([dq, dk, dv], axis=1)
    normed_part = dot(joined_grad, whole_in, NT).astype(bf16)
    first_grad = pair_sum(normed_part)
    order_a, order_b = orders(size)
    attn_shard_grad = scatter(
        [
            grad_halves([(normed, dq, 0, width), (normed, dk, 0, width)], order_a, size, me),
            grad_halves([(normed, dv, 0, width), (attn_low, mixed, 0, width)], order_b, size, me),
        ],
        size,
    )
    input_shard = attn_shard_grad[:, : 3 * width].reshape(rows, 3, width)
    output_shard = attn_shard_grad[:, 3 * width :]
    first_norm_grad, gain_one, shift_one = norm_backward(first_grad, unit_one, scale_one, norm_params[:, 0])
    input_grad = hidden_grad + first_norm_grad

    vectors = jnp.concatenate(
        [gain_one, shift_one, gain_two, shift_two, freq_grad.reshape(-1)], axis=0
    ).reshape(-1, LANES)
    vectors = butterfly(vectors, size).reshape(-1)
    count = gain_one.shape[0]
    vector_sum = vectors[: 4 * count].reshape(4, count).T
    freq_sum = vectors[4 * count :].reshape(2, heads, half)
    partial_squares = (
        jnp.sum(input_shard * input_shard)
        + jnp.sum(output_shard * output_shard)
        + jnp.sum(expand_shard * expand_shard)
        + jnp.sum(reduce_shard * reduce_shard)
    )
    partial_squares = partial_squares + lead_data * (
        lead_model * jnp.sum(vector_sum * vector_sum) + jnp.sum(freq_sum * freq_sum)
    )
    squares = partial_squares + lax.ppermute(partial_squares, "mp", [(0, 1), (1, 0)])
    clip_norm = jnp.sqrt(butterfly(squares, size))
    factor = jnp.minimum(1.0, clip_limit / clip_norm)
    first_input, second_input, updated_input = adamw(
        input_proj, input_first, input_second, input_shard * factor, matrix_rate, matrix_decay
    )
    first_output, second_output, updated_output = adamw(
        output_proj, output_first, output_second, output_shard * factor, matrix_rate, matrix_decay
    )
    first_expand, second_expand, updated_expand = adamw(
        expand_proj, expand_first, expand_second, expand_shard * factor, matrix_rate, matrix_decay
    )
    first_reduce, second_reduce, updated_reduce = adamw(
        reduce_proj, reduce_first, reduce_second, reduce_shard * factor, matrix_rate, matrix_decay
    )
    first_norm, second_norm, updated_norm = adamw(
        norm_params, norm_first, norm_second, vector_sum * factor, vector_rate, 0.0
    )
    first_rope, second_rope, updated_rope = adamw(
        rope_freqs, rope_first, rope_second, freq_sum * factor, vector_rate, 0.0
    )
    return (
        activations,
        input_grad,
        clip_norm,
        first_input,
        second_input,
        updated_input,
        first_output,
        second_output,
        updated_output,
        first_expand,
        second_expand,
        updated_expand,
        first_reduce,
        second_reduce,
        updated_reduce,
        first_norm,
        second_norm,
        updated_norm,
        first_rope,
        second_rope,
        updated_rope,
    )


def solution(mesh):
    rows, cube, flat, full = P("dp", None), P("dp", None, "mp"), P("dp", "mp"), P()
    rope = P(None, "mp", None)
    in_specs = (
        (rows, rows, P("dp"), cube, flat, flat, flat, full, rope)
        + (cube, cube)
        + (flat,) * 6
        + (full, full, rope, rope)
    )
    out_specs = (rows, rows, full) + (cube,) * 3 + (flat,) * 9 + (full,) * 3 + (rope,) * 3
    return jax.shard_map(
        partial(local, mesh.shape["dp"]), mesh=mesh, in_specs=in_specs, out_specs=out_specs, check_vma=False
    )
```

```python
import jax
import jax.numpy as jnp
from jax import lax
from jax.experimental import pallas as pl
from jax.experimental.pallas import tpu as pltpu
from jax.sharding import PartitionSpec as P


HD = 64
SIDES = (14, 20, 24)
STEP = 10
TOK_DEV = 1536

norm_epsilon = 1e-06
adam_epsilon = 1e-08
beta_first = 0.9
beta_second = 0.999
clip_limit = 1.0
matrix_rate = 0.05
matrix_decay = 0.05
vector_rate = 0.5

bf16 = jnp.bfloat16
f32 = jnp.float32
NT = (((1,), (1,)), ((), ()))
NN = (((1,), (0,)), ((), ()))
TN = (((0,), (0,)), ((), ()))
LANES = 128
MIB = 1024 * 1024


def dot(a, b, dims):
    return lax.dot_general(a, b, dims, preferred_element_type=f32)


def swap(value, axis, size, bit):
    return lax.ppermute(value, axis, [(i, i ^ bit) for i in range(size)])


def bits_of(size):
    return [1 << b for b in reversed(range(size.bit_length() - 1))]


def orders(size):
    bits = bits_of(size)
    return (bits, bits[:-2] + [bits[-1], bits[-2]])


def masks_of(order):
    masks = [0]
    for bit in order:
        masks = masks + [m ^ bit for m in masks]
    return masks


def tie(value, *others):
    return lax.optimization_barrier((value,) + others)[0]


def gather_far(shard, size):
    cur = shard[None]
    for bit in bits_of(size)[:-2]:
        cur = jnp.concatenate([cur, swap(cur, "dp", size, bit)], axis=0)
    return cur


def gather_near(cur, size):
    half = cur.shape[2] // 2
    parts = [cur[:, :, color * half : (color + 1) * half] for color in range(2)]
    for color, order in enumerate(orders(size)):
        parts[color] = jnp.concatenate(
            [parts[color], swap(parts[color], "dp", size, order[-2])], axis=0
        )
    out = []
    for color, order in enumerate(orders(size)):
        out.append((parts[color], swap(parts[color], "dp", size, order[-1])))
    return out


def whole(pieces, size, me):
    rows, half = pieces[0][0].shape[1:]
    masks = [masks_of(order) for order in orders(size)]
    if rows % 16:
        cols = []
        for (low, high), ms in zip(pieces, masks):
            place = [0] * size
            for at, m in enumerate(ms):
                place[m] = at
            both = jnp.concatenate([low, high], axis=0)
            index = jnp.array(place, jnp.int32)[jnp.arange(size, dtype=jnp.int32) ^ me]
            cols.append(jnp.take(both, index, axis=0).reshape(size * rows, half))
        return jnp.concatenate(cols, axis=1)

    def kernel(me_ref, a0, a1, b0, b1, out):
        own = me_ref[0]
        for color, pair in enumerate(((a0, a1), (b0, b1))):
            for j, mask in enumerate(masks[color]):
                src = pair[j // (size // 2)]
                at = pl.multiple_of((own ^ mask) * rows, 16)
                out[pl.ds(at, rows), color * half : (color + 1) * half] = src[j % (size // 2)]

    flat = [p for pair in pieces for p in pair]
    return pl.pallas_call(
        kernel,
        out_shape=jax.ShapeDtypeStruct((size * rows, 2 * half), bf16),
        grid_spec=pltpu.PrefetchScalarGridSpec(
            num_scalar_prefetch=1,
            grid=(1,),
            in_specs=[pl.BlockSpec(p.shape, lambda i, c: (0, 0, 0)) for p in flat],
            out_specs=pl.BlockSpec((size * rows, 2 * half), lambda i, c: (0, 0)),
        ),
        compiler_params=pltpu.CompilerParams(vmem_limit_bytes=16 * MIB),
        name="whole",
    )(me[None], *flat)


def grad_halves(terms, order, size, me, total=None, at=0, into=()):
    ms = masks_of(order)
    count = size // 2
    feats = terms[0][0].shape[1]
    rows = feats // size
    width = sum(w for _, _, _, w in terms)
    total = total or width
    if rows % 16:
        mat = jnp.concatenate(
            [dot(l, r[:, c * w : (c + 1) * w], TN) for l, r, c, w in terms], axis=1
        ).reshape(size, rows, width)
        mat = jnp.take(mat, jnp.array(ms, jnp.int32) ^ me, axis=0)
        halves = (mat[:count], mat[count:].astype(bf16))
        return tuple(jnp.concatenate([a, b], axis=2) for a, b in zip(into, halves)) if into else halves

    def kernel(me_ref, *refs):
        ins, (keep, send, acc) = refs[: 2 * len(terms)], refs[2 * len(terms) + len(into) :]
        own = me_ref[0]
        col = 0
        for t, (_, _, _, w) in enumerate(terms):
            acc[:, col : col + w] = dot(ins[2 * t][...], ins[2 * t + 1][...], TN)
            col += w
        for j, mask in enumerate(ms):
            block = acc[pl.ds(pl.multiple_of((own ^ mask) * rows, 16), rows), :]
            if j < count:
                keep[j] = block
            else:
                send[j - count] = block.astype(bf16)

    in_specs, args = [], []
    for l, r, c, w in terms:
        in_specs.append(pl.BlockSpec(l.shape, lambda i, m: (0, 0)))
        in_specs.append(pl.BlockSpec((r.shape[0], w), lambda i, m, c=c: (0, c)))
        args += [l, r]
    aliases = {1 + len(args) + k: k for k in range(len(into))}
    in_specs += [pl.BlockSpec(memory_space=pl.ANY)] * len(into)
    flops = sum(2 * l.shape[0] * l.shape[1] * w for l, _, _, w in terms)
    return pl.pallas_call(
        kernel,
        out_shape=(
            jax.ShapeDtypeStruct((count, rows, total), f32),
            jax.ShapeDtypeStruct((count, rows, total), bf16),
        ),
        grid_spec=pltpu.PrefetchScalarGridSpec(
            num_scalar_prefetch=1,
            grid=(1,),
            in_specs=in_specs,
            out_specs=[pl.BlockSpec((count, rows, width), lambda i, m: (0, 0, at // width))] * 2,
            scratch_shapes=[pltpu.VMEM((feats, width), f32)],
        ),
        input_output_aliases=aliases,
        compiler_params=pltpu.CompilerParams(vmem_limit_bytes=28 * MIB),
        cost_estimate=pl.CostEstimate(flops=flops, transcendentals=0, bytes_accessed=12 * MIB),
        name="grad_halves",
    )(me[None], *args, *into)


def scatter(halves, size):
    totals = []
    for color, order in enumerate(orders(size)):
        keep, send = halves[color]
        totals.append(keep + swap(send, "dp", size, order[-1]).astype(f32))
    parts = []
    for color, order in enumerate(orders(size)):
        total = totals[color]
        count = total.shape[0] // 2
        got = swap(total[count:].astype(bf16), "dp", size, order[-2])
        parts.append(total[:count] + got.astype(f32))
    total = jnp.concatenate(parts, axis=2)
    for bit in bits_of(size)[:-2][::-1]:
        count = total.shape[0] // 2
        total = total[:count] + swap(total[count:].astype(bf16), "dp", size, bit).astype(f32)
    return total[0]


def traded(part):
    return lax.ppermute(part, "mp", [(0, 1), (1, 0)])


def butterfly(value, size):
    for bit in bits_of(size)[::-1]:
        value = value + swap(value, "dp", size, bit)
    return value


def call(kernel, grid, in_specs, out_specs, out_shape, flops, bytes_accessed, vmem, scratch=(), prefetch=0, exps=0, aliases=None):
    return pl.pallas_call(
        kernel,
        out_shape=out_shape,
        grid_spec=pltpu.PrefetchScalarGridSpec(
            num_scalar_prefetch=prefetch,
            grid=grid,
            in_specs=in_specs,
            out_specs=out_specs,
            scratch_shapes=scratch,
        ),
        input_output_aliases=aliases or {},
        compiler_params=pltpu.CompilerParams(vmem_limit_bytes=vmem * MIB),
        cost_estimate=pl.CostEstimate(
            flops=int(flops), transcendentals=int(exps), bytes_accessed=int(bytes_accessed)
        ),
    )


def shape(rows, cols, kind):
    return jax.ShapeDtypeStruct((rows, cols), kind)


def rows_spec(block, cols, at=0):
    return pl.BlockSpec((block, cols), lambda i, *_: (i, at))


def fixed_spec(rows, cols, at=0):
    return pl.BlockSpec((rows, cols), lambda i, *_: (0, at))


def partner(values):
    half, width = HD // 2, values.shape[1]
    lane = lax.broadcasted_iota(jnp.int32, (1, width), 1)
    return jnp.where(lane % HD < half, pltpu.roll(values, width - half, 1), pltpu.roll(values, half, 1))


def project(normed, weights, cosine, sine, width):
    tokens, feats = normed.shape
    block = 256

    def kernel(a_ref, w_ref, cos_ref, sin_ref, out):
        joined = dot(a_ref[...], w_ref[...], NN)
        cos, sin = cos_ref[...], sin_ref[...]
        query, key = joined[:, :width], joined[:, width : 2 * width]
        query = query * cos + partner(query) * sin
        out[:, :width] = (query * 0.125).astype(bf16)
        out[:, width : 2 * width] = (key * cos + partner(key) * sin).astype(bf16)
        out[:, 2 * width :] = joined[:, 2 * width :].astype(bf16)

    return call(
        kernel,
        (tokens // block,),
        [rows_spec(block, feats), fixed_spec(feats, 3 * width), rows_spec(block, width), rows_spec(block, width)],
        rows_spec(block, 3 * width),
        shape(tokens, 3 * width, bf16),
        6 * tokens * feats * width,
        13 * MIB,
        20,
    )(normed, weights, cosine, sine)


def images(level):
    patches = SIDES[level] ** 2
    out = []
    for i in range(-(-TOK_DEV // patches)):
        first, last = i * patches, min((i + 1) * patches, TOK_DEV)
        at, end = first // 16 * 16, -(-last // 16) * 16
        out.append((at, end - at, first - at, last - at))
    return out


def heads_of(block):
    lane = lax.broadcasted_iota(jnp.int32, block.shape, 1)
    zero = jnp.zeros_like(block)
    return jnp.where(lane < HD, block, zero), jnp.where(lane < HD, zero, block)


def attend_kernel(level_ref, q_ref, k_ref, v_ref, o_ref, wide_ref, lse_ref, stat_ref):
    def image(at, window, lo, hi):
        masked = lo != 0 or hi != window
        rows = pl.ds(at, window)
        keys, values = k_ref[rows, :], v_ref[rows, :]
        mixes, stats = [], []
        for head in heads_of(q_ref[rows, :]):
            scores = dot(head, keys, NT)
            if masked:
                place = lax.broadcasted_iota(jnp.int32, scores.shape, 1)
                scores = jnp.where((place >= lo) & (place < hi), scores, -1e30)
            peak = jnp.max(scores, axis=-1, keepdims=True)
            expo = jnp.exp(scores - peak)
            total = jnp.sum(expo, axis=-1, keepdims=True)
            mixes.append(dot(expo.astype(bf16), values, NN) / total)
            stats.append(peak + jnp.log(total))
        lane = lax.broadcasted_iota(jnp.int32, mixes[0].shape, 1)
        mix = jnp.where(lane < HD, mixes[0], mixes[1])
        stat = jnp.where(lane < HD, stats[0], stats[1])
        if masked:
            place = lax.broadcasted_iota(jnp.int32, mix.shape, 0)
            own = (place >= lo) & (place < hi)
            mix = jnp.where(own, mix, wide_ref[rows, :])
            stat = jnp.where(own, stat, stat_ref[rows, :])
        wide_ref[rows, :] = mix
        stat_ref[rows, :] = stat

    for level in range(3):

        @pl.when(level_ref[0] == level)
        def _(level=level):
            for one in images(level):
                image(*one)

    o_ref[...] = wide_ref[...].astype(bf16)
    turned = stat_ref[...].T
    lse_ref[0, 0:1, :] = turned[0:1]
    lse_ref[0, 1:2, :] = turned[HD : HD + 1]


def pair_spec(tokens, at):
    return pl.BlockSpec((tokens, LANES), lambda p, *_: (0, at + p))


def attend(level, qkv, pairs):
    tokens = qkv.shape[0]
    stats = pl.BlockSpec((1, 2, tokens), lambda p, *_: (p, 0, 0))
    return call(
        attend_kernel,
        (pairs,),
        [pair_spec(tokens, 0), pair_spec(tokens, pairs), pair_spec(tokens, 2 * pairs)],
        [pair_spec(tokens, 0), pair_spec(tokens, 0), stats],
        (
            shape(tokens, pairs * LANES, bf16),
            shape(tokens, pairs * LANES, f32),
            jax.ShapeDtypeStruct((pairs, 2, tokens), f32),
        ),
        8e9,
        9 * MIB,
        20,
        [pltpu.VMEM((tokens, LANES), f32)],
        1,
        5e6,
    )(level, qkv, qkv, qkv)


def attend_back_kernel(
    level_ref, q_ref, k_ref, v_ref, do_ref, wide_ref, lse_ref, cos_ref, sin_ref, col_ref, row_ref, *refs
):
    dq_ref, dk_ref, dv_ref, freq_ref, dq_acc, dk_acc, dv_acc, inner_ref = refs[-8:]
    tokens = q_ref.shape[0]
    lane = lax.broadcasted_iota(jnp.int32, (8, LANES), 1)
    line = lax.broadcasted_iota(jnp.int32, (8, LANES), 0)
    pick = jnp.where(lane // HD == line, 1.0, 0.0).astype(f32)
    step = 256
    for at in range(0, tokens, step):
        inner_ref[:, at : at + step] = lax.dot_general(
            pick,
            do_ref[at : at + step, :].astype(f32) * wide_ref[at : at + step, :],
            NT,
            precision=lax.Precision.HIGHEST,
            preferred_element_type=f32,
        )

    def lanes_from(values, at, window):
        return (pltpu.roll(values, tokens - at, 1) if at else values)[:, :window]

    def image(at, window, lo, hi):
        masked = lo != 0 or hi != window
        rows = pl.ds(at, window)
        queries, grads = heads_of(q_ref[rows, :]), heads_of(do_ref[rows, :])
        keys, values = k_ref[rows, :], v_ref[rows, :]
        lse, inner = lanes_from(lse_ref[0], at, window), lanes_from(inner_ref[...], at, window)
        dq, dk, dv = [], [], []
        for h, key in enumerate(heads_of(keys)):
            probs = jnp.exp(dot(keys, queries[h], NT) - lse[h : h + 1])
            if masked:
                place = lax.broadcasted_iota(jnp.int32, probs.shape, 0)
                asked = lax.broadcasted_iota(jnp.int32, probs.shape, 1)
                own = (place >= lo) & (place < hi) & (asked >= lo) & (asked < hi)
                probs = jnp.where(own, probs, 0.0)
            low = (probs * (dot(values, grads[h], NT) - inner[h : h + 1])).astype(bf16)
            dv.append(dot(probs.astype(bf16), grads[h], NN))
            dk.append(dot(low, queries[h], NN))
            dq.append(dot(low, key, TN))
        for acc, parts in ((dq_acc, dq), (dk_acc, dk), (dv_acc, dv)):
            total = parts[0] + parts[1]
            acc[rows, :] = acc[rows, :] + total if masked else total

    for level in range(3):

        @pl.when(level_ref[0] == level)
        def _(level=level):
            if any(lo != 0 or hi != window for _, window, lo, hi in images(level)):
                for acc in (dq_acc, dk_acc, dv_acc):
                    acc[...] = jnp.zeros_like(acc)
            for one in images(level):
                image(*one)

    freq_ref[...] = jnp.zeros_like(freq_ref)

    def finish(c, carry):
        rows = pl.ds(pl.multiple_of(c * step, step), step)
        cosine, sine = cos_ref[rows, :], sin_ref[rows, :]
        dq, dk = dq_acc[rows, :] * 0.125, dk_acc[rows, :]
        dq_other, dk_other = partner(dq), partner(dk)
        dq_ref[rows, :] = (dq * cosine - dq_other * sine).astype(bf16)
        dk_ref[rows, :] = (dk * cosine - dk_other * sine).astype(bf16)
        dv_ref[rows, :] = dv_acc[rows, :].astype(bf16)
        turn = q_ref[rows, :].astype(f32) * 8.0 * dq_other + k_ref[rows, :].astype(f32) * dk_other
        freq_ref[0, 0:1, :] += jnp.sum(col_ref[rows, :] * turn, axis=0, keepdims=True)
        freq_ref[0, 1:2, :] += jnp.sum(row_ref[rows, :] * turn, axis=0, keepdims=True)
        return carry

    lax.fori_loop(0, tokens // step, finish, 0)


def attend_back(level, qkv, mixed_grad, wide, lse, cosine, sine, column, row_pos, pairs, first, last, into=()):
    tokens = qkv.shape[0]
    own = pair_spec(tokens, first)
    pair_rows = pl.BlockSpec((1, 2, tokens), lambda p, *_: (first + p, 0, 0))
    freqs = pl.BlockSpec((1, 2, LANES), lambda p, *_: (first + p, 0, 0))
    fixed = fixed_spec(tokens, LANES)
    out = shape(tokens, pairs * LANES, bf16)
    return call(
        attend_back_kernel,
        (last - first,),
        [own, pair_spec(tokens, pairs + first), pair_spec(tokens, 2 * pairs + first)]
        + [own, own, pair_rows, own, own, fixed, fixed]
        + [pl.BlockSpec(memory_space=pl.ANY)] * len(into),
        [own, own, own, freqs],
        (out, out, out, jax.ShapeDtypeStruct((pairs, 2, LANES), f32)),
        7e9 * (last - first),
        5 * MIB * (last - first),
        32,
        [pltpu.VMEM((tokens, LANES), f32)] * 3 + [pltpu.VMEM((8, tokens), f32)],
        1,
        2e6 * (last - first),
        {11 + k: k for k in range(len(into))},
    )(level, qkv, qkv, qkv, mixed_grad, wide, lse, cosine, sine, column, row_pos, *into)


def norm_rows(values):
    center = values - jnp.mean(values, axis=-1, keepdims=True)
    scale = lax.rsqrt(jnp.mean(center * center, axis=-1, keepdims=True) + norm_epsilon)
    return center * scale, scale


def norm_rows_back(grad, unit, scale, gain):
    scaled = grad * gain
    return scale * (
        scaled
        - jnp.mean(scaled, axis=-1, keepdims=True)
        - unit * jnp.mean(scaled * unit, axis=-1, keepdims=True)
    )


def widen(tokens_in, mine, theirs, gains, weights):
    tokens, feats = tokens_in.shape
    hid = weights.shape[1]
    block = 256

    def kernel(x_ref, mine_ref, theirs_ref, gains_ref, w_ref, hidden_ref, low_ref, z_ref, slope_ref):
        hidden = x_ref[...].astype(f32) + (mine_ref[...].astype(f32) + theirs_ref[...].astype(f32))
        hidden_ref[...] = hidden
        unit, _ = norm_rows(hidden)
        low = (unit * gains_ref[2:3, :] + gains_ref[3:4, :]).astype(bf16)
        low_ref[...] = low
        step = 512
        for at in range(0, hid, step):
            u = dot(low, w_ref[:, at : at + step], NN)
            below = 0.5 * (1.0 + lax.erf(u * (0.5**0.5)))
            z_ref[:, at : at + step] = (u * below).astype(bf16)
            slope = below + u * jnp.exp(-0.5 * u * u) * 0.3989422804014327
            slope_ref[:, at : at + step] = slope.astype(bf16)

    own = rows_spec(block, feats)
    return call(
        kernel,
        (tokens // block,),
        [own, own, own, fixed_spec(4, feats), fixed_spec(feats, hid)],
        [own, own, rows_spec(block, hid), rows_spec(block, hid)],
        (shape(tokens, feats, f32), shape(tokens, feats, bf16), shape(tokens, hid, bf16), shape(tokens, hid, bf16)),
        2 * tokens * feats * hid,
        24 * MIB,
        24,
        exps=5e6,
    )(tokens_in, mine, theirs, gains, weights)


def narrow(upstream, slope, reduce_w, expand_w):
    tokens, feats = upstream.shape
    hid = slope.shape[1]
    block = 256

    def kernel(up_ref, slope_ref, rw_ref, ew_ref, du_ref, db_ref):
        du = (dot(up_ref[...], rw_ref[...], NN) * slope_ref[...].astype(f32)).astype(bf16)
        du_ref[...] = du
        db_ref[...] = dot(du, ew_ref[...], NT).astype(bf16)

    own, wide = rows_spec(block, feats), rows_spec(block, hid)
    fixed = fixed_spec(feats, hid)
    return call(
        kernel,
        (tokens // block,),
        [own, wide, fixed, fixed],
        [wide, own],
        (shape(tokens, hid, bf16), shape(tokens, feats, bf16)),
        4 * tokens * feats * hid,
        20 * MIB,
        24,
    )(upstream, slope, reduce_w, expand_w)


def times_columns(left, right, width, at):
    tokens, feats = left.shape[0], right.shape[0]
    block = 512

    def kernel(l_ref, r_ref, out):
        out[...] = dot(l_ref[...], r_ref[...], NT).astype(bf16)

    return call(
        kernel,
        (tokens // block,),
        [rows_spec(block, width), fixed_spec(feats, width, at)],
        rows_spec(block, feats),
        shape(tokens, feats, bf16),
        2 * tokens * feats * width,
        9 * MIB,
        20,
    )(left, right)


def second_back(upstream, mine, theirs, hidden, gains, weights, width, at):
    tokens, feats = upstream.shape
    block = 256

    def kernel(up_ref, mine_ref, theirs_ref, hidden_ref, gains_ref, w_ref, grad_ref, low_ref, do_ref, sums_ref):
        grad = mine_ref[...].astype(f32) + theirs_ref[...].astype(f32)
        unit, scale = norm_rows(hidden_ref[...])
        total = up_ref[...].astype(f32) + norm_rows_back(grad, unit, scale, gains_ref[2:3, :])
        grad_ref[...] = total
        low = total.astype(bf16)
        low_ref[...] = low
        do_ref[...] = dot(low, w_ref[...], NN).astype(bf16)

        @pl.when(pl.program_id(0) == 0)
        def _():
            sums_ref[...] = jnp.zeros_like(sums_ref)

        sums_ref[0:1, :] += jnp.sum(grad * unit, axis=0, keepdims=True)
        sums_ref[1:2, :] += jnp.sum(grad, axis=0, keepdims=True)

    own = rows_spec(block, feats)
    return call(
        kernel,
        (tokens // block,),
        [own, own, own, own, fixed_spec(4, feats), fixed_spec(feats, width, at)],
        [own, own, rows_spec(block, width), fixed_spec(2, feats)],
        (shape(tokens, feats, f32), shape(tokens, feats, bf16), shape(tokens, width, bf16), shape(2, feats, f32)),
        2 * tokens * feats * width,
        24 * MIB,
        20,
    )(upstream, mine, theirs, hidden, gains, weights)


def first_share(dq, dk, dv, weights):
    tokens, width = dq.shape
    feats = weights.shape[0]
    block = 256

    def kernel(dq_ref, dk_ref, dv_ref, w_ref, out):
        total = dot(dq_ref[...], w_ref[:, :width], NT)
        total = total + dot(dk_ref[...], w_ref[:, width : 2 * width], NT)
        out[...] = (total + dot(dv_ref[...], w_ref[:, 2 * width :], NT)).astype(bf16)

    own = rows_spec(block, width)
    return call(
        kernel,
        (tokens // block,),
        [own, own, own, fixed_spec(feats, 3 * width)],
        rows_spec(block, feats),
        shape(tokens, feats, bf16),
        6 * tokens * feats * width,
        8 * MIB,
        16,
    )(dq, dk, dv, weights)


def first_back(tokens_in, mine, theirs, hidden_grad, gains):
    tokens, feats = tokens_in.shape
    block = 256

    def kernel(x_ref, mine_ref, theirs_ref, hidden_ref, gains_ref, grad_ref, sums_ref):
        grad = mine_ref[...].astype(f32) + theirs_ref[...].astype(f32)
        unit, scale = norm_rows(x_ref[...].astype(f32))
        grad_ref[...] = hidden_ref[...] + norm_rows_back(grad, unit, scale, gains_ref[0:1, :])

        @pl.when(pl.program_id(0) == 0)
        def _():
            sums_ref[...] = jnp.zeros_like(sums_ref)

        sums_ref[0:1, :] += jnp.sum(grad * unit, axis=0, keepdims=True)
        sums_ref[1:2, :] += jnp.sum(grad, axis=0, keepdims=True)

    own = rows_spec(block, feats)
    return call(
        kernel,
        (tokens // block,),
        [own, own, own, own, fixed_spec(4, feats)],
        [own, fixed_spec(2, feats)],
        (shape(tokens, feats, f32), shape(2, feats, f32)),
        20 * tokens * feats,
        20 * MIB,
        20,
    )(tokens_in, mine, theirs, hidden_grad, gains)


def slab_layout(resolution):
    places = jnp.arange(TOK_DEV, dtype=jnp.int32)
    side_len = jnp.where(
        resolution == 0, SIDES[0], jnp.where(resolution == 1, SIDES[1], SIDES[2])
    ).astype(jnp.int32)
    patches = side_len * side_len
    image_id = places // patches
    within = places % patches
    column = (within % side_len).astype(f32)
    row_pos = (within // side_len).astype(f32)
    usable = (image_id < TOK_DEV // patches).astype(f32)
    return (column, row_pos, usable)


def norm_forward(values, gain_vec, shift_vec):
    center = values - jnp.mean(values, axis=-1, keepdims=True)
    spread = jnp.mean(center * center, axis=-1, keepdims=True)
    scale_rows = lax.rsqrt(spread + norm_epsilon)
    unit_rows = center * scale_rows
    return (unit_rows * gain_vec + shift_vec, unit_rows, scale_rows)


def adamw(weight, first, second, gradient, rate, decay):
    first = beta_first * first + (1.0 - beta_first) * gradient
    second = beta_second * second + (1.0 - beta_second) * gradient * gradient
    first_fix = 1.0 - beta_first**STEP
    second_fix = 1.0 - beta_second**STEP
    update = first / first_fix / (jnp.sqrt(second / second_fix) + adam_epsilon)
    return (first, second, weight - rate * (update + decay * weight))


def step_kernel(*refs):
    squares, refs = refs[0], refs[1:]
    states, grads = refs[:18], refs[18:24]
    clip_ref, outs = refs[24], refs[25:]
    clip = jnp.sqrt(squares[...])
    clip_ref[...] = clip
    factor = jnp.minimum(1.0, clip_limit / clip)
    for p in range(6):
        rate, decay = (matrix_rate, matrix_decay) if p < 4 else (vector_rate, 0.0)
        weight, first, second = states[3 * p : 3 * p + 3]
        results = outs[3 * p : 3 * p + 3]
        if p == 0:
            width = weight.shape[2]
            for k in range(weight.shape[0]):
                grad = grads[0][:, k * width : (k + 1) * width] * factor
                for out, value in zip(results, adamw(weight[k], first[k], second[k], grad, rate, decay)):
                    out[k] = value
            continue
        if weight.ndim == 3:
            grad = grads[p][...] * factor[None]
        else:
            grad = grads[p][...] * factor
        for out, value in zip(results, adamw(weight[...], first[...], second[...], grad, rate, decay)):
            out[...] = value


def optimize(squares, states, grads):
    outs = tuple(jax.ShapeDtypeStruct(a.shape, f32) for a in states)
    return pl.pallas_call(
        step_kernel,
        out_shape=(jax.ShapeDtypeStruct((1, 1), f32),) + outs,
        compiler_params=pltpu.CompilerParams(vmem_limit_bytes=24 * MIB),
        name="optimize",
    )(squares.reshape(1, 1), *states, *grads)


def local(
    size,
    tokens,
    cotangent,
    device_class,
    input_proj,
    output_proj,
    expand_proj,
    reduce_proj,
    norm_params,
    rope_freqs,
    input_first,
    input_second,
    output_first,
    output_second,
    expand_first,
    expand_second,
    reduce_first,
    reduce_second,
    norm_first,
    norm_second,
    rope_first,
    rope_second,
):
    heads = rope_freqs.shape[1]
    width = heads * HD
    pairs = width // LANES
    me = lax.axis_index("dp").astype(jnp.int32)
    lead_data = (me == 0).astype(f32)
    lead_model = (lax.axis_index("mp") == 0).astype(f32)
    rows = input_proj.shape[0]

    attn_shard = jnp.concatenate(
        [input_proj.reshape(rows, 3 * width).astype(bf16), output_proj.astype(bf16)], axis=1
    )
    attn_far = gather_far(attn_shard, size)
    attn_pieces = gather_near(attn_far, size)
    expand_far = gather_far(tie(expand_proj.astype(bf16), attn_far), size)
    expand_pieces = gather_near(tie(expand_far, *attn_pieces[0], *attn_pieces[1]), size)
    reduce_far = gather_far(tie(reduce_proj.astype(bf16), expand_far), size)
    reduce_pieces = gather_near(tie(reduce_far, *expand_pieces[0], *expand_pieces[1]), size)

    column, row_pos, usable = slab_layout(device_class[0])
    gains = norm_params.T
    normed = norm_forward(tokens.astype(f32), norm_params[:, 0], norm_params[:, 1])[0].astype(bf16)
    half = HD // 2
    freqs = jnp.concatenate([rope_freqs, rope_freqs], axis=2).reshape(2, width)
    angles = column[:, None] * freqs[0][None] + row_pos[:, None] * freqs[1][None]
    cosine = jnp.cos(angles)
    sine = jnp.sin(angles) * jnp.where(jnp.arange(width) % HD < half, -1.0, 1.0)[None]
    column = jnp.broadcast_to(column[:, None], (TOK_DEV, LANES))
    row_pos = jnp.broadcast_to(row_pos[:, None], (TOK_DEV, LANES))
    upstream = (cotangent.astype(f32) * usable[:, None]).astype(bf16)

    def product(terms, color, *place):
        return grad_halves(terms, orders(size)[color], size, me, *place)

    attn_whole = whole(attn_pieces, size, me)
    qkv = project(normed, attn_whole, cosine, sine, width)
    mixed, mixed_wide, lse = attend(device_class, qkv, pairs)
    attn_part = times_columns(mixed, attn_whole, width, 3)
    attn_other = traded(attn_part)
    whole_expand = whole(expand_pieces, size, me)
    hidden_rows, second_in, activ, slope = widen(tokens, attn_part, attn_other, gains, whole_expand)
    wide = activ.shape[1] // 2
    reduce_halves = [product([(upstream, activ, c, wide)], c) for c in range(2)]
    reduce_shard = scatter(reduce_halves, size)
    whole_reduce = whole(reduce_pieces, size, me)
    expanded_low, second_part = narrow(upstream, slope, whole_reduce, whole_expand)
    second_other = traded(second_part)
    lead = width - LANES
    cuts = (wide + lead, wide + LANES)
    expand_halves = [product([(second_in, expanded_low, c, wide)], c, cuts[c]) for c in range(2)]
    hidden_grad, attn_low, mixed_low, sums_two = second_back(
        upstream, second_part, second_other, hidden_rows, gains, attn_whole, width, 3
    )
    expand_halves = [
        product([(attn_low, mixed, 0, lead)], 0, cuts[0], wide, expand_halves[0]),
        product([(attn_low, mixed, lead // LANES, LANES)], 1, cuts[1], wide, expand_halves[1]),
    ]
    both = scatter(expand_halves, size)
    expand_shard = jnp.concatenate([both[:, :wide], both[:, cuts[0] : cuts[0] + wide]], axis=1)
    output_shard = jnp.concatenate([both[:, wide : cuts[0]], both[:, cuts[0] + wide :]], axis=1)
    back = (device_class, qkv, mixed_low, mixed_wide, lse, cosine, sine, column, row_pos, pairs)
    done = attend_back(*back, 0, pairs - 1)
    dq, dk, dv, turn = attend_back(*back, pairs - 1, pairs, done)
    freq_grad = turn.transpose(1, 0, 2).reshape(2, heads, HD)
    freq_grad = freq_grad[:, :, :half] - freq_grad[:, :, half:]
    input_halves = [
        product([(normed, dq, 0, width), (normed, dk, 0, lead)], 0),
        product([(normed, dk, lead // LANES, LANES), (normed, dv, 0, width)], 1),
    ]
    input_shard = scatter(input_halves, size)
    first_part = first_share(dq, dk, dv, attn_whole)
    first_other = traded(first_part)
    input_grad, sums_one = first_back(tokens, first_part, first_other, hidden_grad, gains)
    mlp_part = times_columns(tie(activ, sums_one), whole_reduce, 2 * wide, 0)
    mlp_other = traded(mlp_part)
    activations = (hidden_rows + (mlp_part.astype(f32) + mlp_other.astype(f32))).astype(bf16)

    vectors = jnp.concatenate(
        [sums_one.reshape(-1), sums_two.reshape(-1), freq_grad.reshape(-1)], axis=0
    ).reshape(-1, LANES)
    vectors = butterfly(vectors, size).reshape(-1)
    count = tokens.shape[1]
    vector_sum = vectors[: 4 * count].reshape(4, count)
    freq_sum = vectors[4 * count :].reshape(2, heads, half)
    partial_squares = (
        jnp.sum(input_shard * input_shard)
        + jnp.sum(output_shard * output_shard)
        + jnp.sum(expand_shard * expand_shard)
        + jnp.sum(reduce_shard * reduce_shard)
    )
    partial_squares = partial_squares + lead_data * (
        lead_model * jnp.sum(vector_sum * vector_sum) + jnp.sum(freq_sum * freq_sum)
    )
    squares = partial_squares + lax.ppermute(partial_squares, "mp", [(0, 1), (1, 0)])
    squares = butterfly(squares, size)

    def flip(value):
        return value.transpose(1, 0, 2)

    states = (
        tuple(flip(a) for a in (input_proj, input_first, input_second))
        + (output_proj, output_first, output_second)
        + (expand_proj, expand_first, expand_second)
        + (reduce_proj, reduce_first, reduce_second)
        + (norm_params.T, norm_first.T, norm_second.T)
        + tuple(flip(a) for a in (rope_freqs, rope_first, rope_second))
    )
    grads = (input_shard, output_shard, expand_shard, reduce_shard, vector_sum, flip(freq_sum))
    clip_norm, *new = optimize(squares, states, grads)
    new = (
        [flip(a) for a in new[:3]]
        + new[3:12]
        + [a.T for a in new[12:15]]
        + [flip(a) for a in new[15:]]
    )
    return (activations, input_grad, clip_norm.reshape(()), *new)


def solution(mesh):
    rows, cube, flat, full = P("dp", None), P("dp", None, "mp"), P("dp", "mp"), P()
    rope = P(None, "mp", None)
    in_specs = (
        (rows, rows, P("dp"), cube, flat, flat, flat, full, rope)
        + (cube, cube)
        + (flat,) * 6
        + (full, full, rope, rope)
    )
    out_specs = (rows, rows, full) + (cube,) * 3 + (flat,) * 9 + (full,) * 3 + (rope,) * 3

    def step(*args):
        return local(mesh.shape["dp"], *args)

    step = jax.shard_map(step, mesh=mesh, in_specs=in_specs, out_specs=out_specs, check_vma=False)
    return step
```

```python
import jax
import jax.numpy as jnp
from jax import lax
from jax.experimental import pallas as pl
from jax.experimental.pallas import tpu as pltpu
from jax.sharding import PartitionSpec as P


HD = 64
SIDES = (14, 20, 24)
STEP = 10
TOK_DEV = 1536

norm_epsilon = 1e-06
adam_epsilon = 1e-08
beta_first = 0.9
beta_second = 0.999
clip_limit = 1.0
matrix_rate = 0.05
matrix_decay = 0.05
vector_rate = 0.5

bf16 = jnp.bfloat16
f32 = jnp.float32
NT = (((1,), (1,)), ((), ()))
NN = (((1,), (0,)), ((), ()))
TN = (((0,), (0,)), ((), ()))
LANES = 128
MIB = 1024 * 1024


def dot(a, b, dims):
    return lax.dot_general(a, b, dims, preferred_element_type=f32)


def swap(value, axis, size, bit):
    return lax.ppermute(value, axis, [(i, i ^ bit) for i in range(size)])


def bits_of(size):
    return [1 << b for b in reversed(range(size.bit_length() - 1))]


def orders(size):
    bits = bits_of(size)
    return (bits, bits[:-2] + [bits[-1], bits[-2]])


def masks_of(order):
    masks = [0]
    for bit in order:
        masks = masks + [m ^ bit for m in masks]
    return masks


def tie(value, *others):
    return lax.optimization_barrier((value,) + others)[0]


def gather_far(shard, size):
    cur = shard[None]
    for bit in bits_of(size)[:-2]:
        cur = jnp.concatenate([cur, swap(cur, "dp", size, bit)], axis=0)
    return cur


def gather_near(cur, size):
    half = cur.shape[2] // 2
    parts = [cur[:, :, color * half : (color + 1) * half] for color in range(2)]
    for color, order in enumerate(orders(size)):
        parts[color] = jnp.concatenate(
            [parts[color], swap(parts[color], "dp", size, order[-2])], axis=0
        )
    out = []
    for color, order in enumerate(orders(size)):
        out.append((parts[color], swap(parts[color], "dp", size, order[-1])))
    return out


def whole(pieces, size, me):
    rows, half = pieces[0][0].shape[1:]
    masks = [masks_of(order) for order in orders(size)]
    if rows % 16:
        cols = []
        for (low, high), ms in zip(pieces, masks):
            place = [0] * size
            for at, m in enumerate(ms):
                place[m] = at
            both = jnp.concatenate([low, high], axis=0)
            index = jnp.array(place, jnp.int32)[jnp.arange(size, dtype=jnp.int32) ^ me]
            cols.append(jnp.take(both, index, axis=0).reshape(size * rows, half))
        return jnp.concatenate(cols, axis=1)

    def kernel(me_ref, a0, a1, b0, b1, out):
        own = me_ref[0]
        for color, pair in enumerate(((a0, a1), (b0, b1))):
            for j, mask in enumerate(masks[color]):
                src = pair[j // (size // 2)]
                at = pl.multiple_of((own ^ mask) * rows, 16)
                out[pl.ds(at, rows), color * half : (color + 1) * half] = src[j % (size // 2)]

    flat = [p for pair in pieces for p in pair]
    return pl.pallas_call(
        kernel,
        out_shape=jax.ShapeDtypeStruct((size * rows, 2 * half), bf16),
        grid_spec=pltpu.PrefetchScalarGridSpec(
            num_scalar_prefetch=1,
            grid=(1,),
            in_specs=[pl.BlockSpec(p.shape, lambda i, c: (0, 0, 0)) for p in flat],
            out_specs=pl.BlockSpec((size * rows, 2 * half), lambda i, c: (0, 0)),
        ),
        compiler_params=pltpu.CompilerParams(vmem_limit_bytes=12 * MIB),
        name="whole",
    )(me[None], *flat)


def grad_halves(terms, order, size, me, total=None, at=0, into=()):
    ms = masks_of(order)
    count = size // 2
    feats = terms[0][0].shape[1]
    rows = feats // size
    width = sum(w for _, _, _, w in terms)
    total = total or width
    if rows % 16:
        mat = jnp.concatenate(
            [dot(l, r[:, c * w : (c + 1) * w], TN) for l, r, c, w in terms], axis=1
        ).reshape(size, rows, width)
        mat = jnp.take(mat, jnp.array(ms, jnp.int32) ^ me, axis=0)
        halves = (mat[:count], mat[count:].astype(bf16))
        return tuple(jnp.concatenate([a, b], axis=2) for a, b in zip(into, halves)) if into else halves

    def kernel(me_ref, *refs):
        ins, (keep, send, acc) = refs[: 2 * len(terms)], refs[2 * len(terms) + len(into) :]
        own = me_ref[0]
        col = 0
        for t, (_, _, _, w) in enumerate(terms):
            acc[:, col : col + w] = dot(ins[2 * t][...], ins[2 * t + 1][...], TN)
            col += w
        for j, mask in enumerate(ms):
            block = acc[pl.ds(pl.multiple_of((own ^ mask) * rows, 16), rows), :]
            if j < count:
                keep[j] = block
            else:
                send[j - count] = block.astype(bf16)

    in_specs, args = [], []
    for l, r, c, w in terms:
        in_specs.append(pl.BlockSpec(l.shape, lambda i, m: (0, 0)))
        in_specs.append(pl.BlockSpec((r.shape[0], w), lambda i, m, c=c: (0, c)))
        args += [l, r]
    aliases = {1 + len(args) + k: k for k in range(len(into))}
    in_specs += [pl.BlockSpec(memory_space=pl.ANY)] * len(into)
    flops = sum(2 * l.shape[0] * l.shape[1] * w for l, _, _, w in terms)
    return pl.pallas_call(
        kernel,
        out_shape=(
            jax.ShapeDtypeStruct((count, rows, total), f32),
            jax.ShapeDtypeStruct((count, rows, total), bf16),
        ),
        grid_spec=pltpu.PrefetchScalarGridSpec(
            num_scalar_prefetch=1,
            grid=(1,),
            in_specs=in_specs,
            out_specs=[pl.BlockSpec((count, rows, width), lambda i, m: (0, 0, at // width))] * 2,
            scratch_shapes=[pltpu.VMEM((feats, width), f32)],
        ),
        input_output_aliases=aliases,
        compiler_params=pltpu.CompilerParams(vmem_limit_bytes=18 * MIB),
        cost_estimate=pl.CostEstimate(flops=flops, transcendentals=0, bytes_accessed=12 * MIB),
        name="grad_halves",
    )(me[None], *args, *into)


def joined(keep, got):
    count = keep.shape[0] // 2
    kept = keep[:count] + got[:count].astype(f32)
    return kept, (keep[count:] + got[count:].astype(f32)).astype(bf16)


def scatter(halves, size):
    halves = list(halves)
    for color, order in enumerate(orders(size)):
        keep, send = halves[color]
        halves[color] = joined(keep, swap(send, "dp", size, order[-1]))
    for color, order in enumerate(orders(size)):
        keep, send = halves[color]
        halves[color] = joined(keep, swap(send, "dp", size, order[-2]))
    keep, send = (jnp.concatenate([halves[0][k], halves[1][k]], axis=2) for k in range(2))
    far = bits_of(size)[:-2][::-1]
    for bit in far[:-1]:
        keep, send = joined(keep, swap(send, "dp", size, bit))
    total = keep + swap(send, "dp", size, far[-1]).astype(f32)
    return total.reshape(total.shape[1:])


def traded(part):
    return lax.ppermute(part, "mp", [(0, 1), (1, 0)])


def butterfly(value, size):
    for bit in bits_of(size)[::-1]:
        value = value + swap(value, "dp", size, bit)
    return value


def call(kernel, grid, in_specs, out_specs, out_shape, flops, bytes_accessed, vmem, scratch=(), prefetch=0, exps=0, aliases=None):
    return pl.pallas_call(
        kernel,
        out_shape=out_shape,
        grid_spec=pltpu.PrefetchScalarGridSpec(
            num_scalar_prefetch=prefetch,
            grid=grid,
            in_specs=in_specs,
            out_specs=out_specs,
            scratch_shapes=scratch,
        ),
        input_output_aliases=aliases or {},
        compiler_params=pltpu.CompilerParams(vmem_limit_bytes=vmem * MIB),
        cost_estimate=pl.CostEstimate(
            flops=int(flops), transcendentals=int(exps), bytes_accessed=int(bytes_accessed)
        ),
    )


def shape(rows, cols, kind):
    return jax.ShapeDtypeStruct((rows, cols), kind)


def rows_spec(block, cols, at=0):
    return pl.BlockSpec((block, cols), lambda i, *_: (i, at))


def fixed_spec(rows, cols, at=0):
    return pl.BlockSpec((rows, cols), lambda i, *_: (0, at))


def partner(values):
    half, width = HD // 2, values.shape[1]
    lane = lax.broadcasted_iota(jnp.int32, (1, width), 1)
    return jnp.where(lane % HD < half, pltpu.roll(values, width - half, 1), pltpu.roll(values, half, 1))


def project(normed, weights, cosine, sine, width):
    tokens, feats = normed.shape
    block = 256

    def kernel(a_ref, w_ref, cos_ref, sin_ref, out):
        joined = dot(a_ref[...], w_ref[...], NN)
        cos, sin = cos_ref[...], sin_ref[...]
        query, key = joined[:, :width], joined[:, width : 2 * width]
        query = query * cos + partner(query) * sin
        out[:, :width] = (query * 0.125).astype(bf16)
        out[:, width : 2 * width] = (key * cos + partner(key) * sin).astype(bf16)
        out[:, 2 * width :] = joined[:, 2 * width :].astype(bf16)

    return call(
        kernel,
        (tokens // block,),
        [rows_spec(block, feats), fixed_spec(feats, 3 * width), rows_spec(block, width), rows_spec(block, width)],
        rows_spec(block, 3 * width),
        shape(tokens, 3 * width, bf16),
        6 * tokens * feats * width,
        13 * MIB,
        14,
    )(normed, weights, cosine, sine)


def images(level):
    patches = SIDES[level] ** 2
    out = []
    for i in range(-(-TOK_DEV // patches)):
        first, last = i * patches, min((i + 1) * patches, TOK_DEV)
        at, end = first // 16 * 16, -(-last // 16) * 16
        out.append((at, end - at, first - at, last - at))
    return out


def heads_of(block):
    lane = lax.broadcasted_iota(jnp.int32, block.shape, 1)
    zero = jnp.zeros_like(block)
    return jnp.where(lane < HD, block, zero), jnp.where(lane < HD, zero, block)


def attend_kernel(level_ref, q_ref, k_ref, v_ref, o_ref, wide_ref, lse_ref, stat_ref):
    def image(at, window, lo, hi):
        masked = lo != 0 or hi != window
        rows = pl.ds(at, window)
        keys, values = k_ref[rows, :], v_ref[rows, :]
        mixes, stats = [], []
        for head in heads_of(q_ref[rows, :]):
            scores = dot(head, keys, NT)
            if masked:
                place = lax.broadcasted_iota(jnp.int32, scores.shape, 1)
                scores = jnp.where((place >= lo) & (place < hi), scores, -1e30)
            peak = jnp.max(scores, axis=-1, keepdims=True)
            expo = jnp.exp(scores - peak)
            total = jnp.sum(expo, axis=-1, keepdims=True)
            mixes.append(dot(expo.astype(bf16), values, NN) / total)
            stats.append(peak + jnp.log(total))
        lane = lax.broadcasted_iota(jnp.int32, mixes[0].shape, 1)
        mix = jnp.where(lane < HD, mixes[0], mixes[1])
        stat = jnp.where(lane < HD, stats[0], stats[1])
        if masked:
            place = lax.broadcasted_iota(jnp.int32, mix.shape, 0)
            own = (place >= lo) & (place < hi)
            mix = jnp.where(own, mix, wide_ref[rows, :])
            stat = jnp.where(own, stat, stat_ref[rows, :])
        wide_ref[rows, :] = mix
        stat_ref[rows, :] = stat

    for level in range(3):

        @pl.when(level_ref[0] == level)
        def _(level=level):
            for one in images(level):
                image(*one)

    o_ref[...] = wide_ref[...].astype(bf16)
    turned = stat_ref[...].T
    lse_ref[0, 0:1, :] = turned[0:1]
    lse_ref[0, 1:2, :] = turned[HD : HD + 1]


def pair_spec(tokens, at):
    return pl.BlockSpec((tokens, LANES), lambda p, *_: (0, at + p))


def attend(level, qkv, pairs):
    tokens = qkv.shape[0]
    stats = pl.BlockSpec((1, 2, tokens), lambda p, *_: (p, 0, 0))
    return call(
        attend_kernel,
        (pairs,),
        [pair_spec(tokens, 0), pair_spec(tokens, pairs), pair_spec(tokens, 2 * pairs)],
        [pair_spec(tokens, 0), pair_spec(tokens, 0), stats],
        (
            shape(tokens, pairs * LANES, bf16),
            shape(tokens, pairs * LANES, f32),
            jax.ShapeDtypeStruct((pairs, 2, tokens), f32),
        ),
        8e9,
        9 * MIB,
        18,
        [pltpu.VMEM((tokens, LANES), f32)],
        1,
        5e6,
    )(level, qkv, qkv, qkv)


def attend_back_kernel(
    level_ref, q_ref, k_ref, v_ref, do_ref, wide_ref, lse_ref, cos_ref, sin_ref, col_ref, row_ref, *refs
):
    dq_ref, dk_ref, dv_ref, freq_ref, dq_acc, dk_acc, dv_acc, inner_ref = refs[-8:]
    tokens = q_ref.shape[0]
    lane = lax.broadcasted_iota(jnp.int32, (8, LANES), 1)
    line = lax.broadcasted_iota(jnp.int32, (8, LANES), 0)
    pick = jnp.where(lane // HD == line, 1.0, 0.0).astype(f32)
    step = 256
    for at in range(0, tokens, step):
        inner_ref[:, at : at + step] = lax.dot_general(
            pick,
            do_ref[at : at + step, :].astype(f32) * wide_ref[at : at + step, :],
            NT,
            precision=lax.Precision.HIGHEST,
            preferred_element_type=f32,
        )

    def lanes_from(values, at, window):
        return (pltpu.roll(values, tokens - at, 1) if at else values)[:, :window]

    def image(at, window, lo, hi):
        masked = lo != 0 or hi != window
        rows = pl.ds(at, window)
        queries, grads = heads_of(q_ref[rows, :]), heads_of(do_ref[rows, :])
        keys, values = k_ref[rows, :], v_ref[rows, :]
        lse, inner = lanes_from(lse_ref[0], at, window), lanes_from(inner_ref[...], at, window)
        dq, dk, dv = [], [], []
        for h, key in enumerate(heads_of(keys)):
            probs = jnp.exp(dot(keys, queries[h], NT) - lse[h : h + 1])
            if masked:
                place = lax.broadcasted_iota(jnp.int32, probs.shape, 0)
                asked = lax.broadcasted_iota(jnp.int32, probs.shape, 1)
                own = (place >= lo) & (place < hi) & (asked >= lo) & (asked < hi)
                probs = jnp.where(own, probs, 0.0)
            low = (probs * (dot(values, grads[h], NT) - inner[h : h + 1])).astype(bf16)
            dv.append(dot(probs.astype(bf16), grads[h], NN))
            dk.append(dot(low, queries[h], NN))
            dq.append(dot(low, key, TN))
        for acc, parts in ((dq_acc, dq), (dk_acc, dk), (dv_acc, dv)):
            total = parts[0] + parts[1]
            acc[rows, :] = acc[rows, :] + total if masked else total

    for level in range(3):

        @pl.when(level_ref[0] == level)
        def _(level=level):
            if any(lo != 0 or hi != window for _, window, lo, hi in images(level)):
                for acc in (dq_acc, dk_acc, dv_acc):
                    acc[...] = jnp.zeros_like(acc)
            for one in images(level):
                image(*one)

    freq_ref[...] = jnp.zeros_like(freq_ref)

    def finish(c, carry):
        rows = pl.ds(pl.multiple_of(c * step, step), step)
        cosine, sine = cos_ref[rows, :], sin_ref[rows, :]
        dq, dk = dq_acc[rows, :] * 0.125, dk_acc[rows, :]
        dq_other, dk_other = partner(dq), partner(dk)
        dq_ref[rows, :] = (dq * cosine - dq_other * sine).astype(bf16)
        dk_ref[rows, :] = (dk * cosine - dk_other * sine).astype(bf16)
        dv_ref[rows, :] = dv_acc[rows, :].astype(bf16)
        turn = q_ref[rows, :].astype(f32) * 8.0 * dq_other + k_ref[rows, :].astype(f32) * dk_other
        freq_ref[0, 0:1, :] += jnp.sum(col_ref[rows, :] * turn, axis=0, keepdims=True)
        freq_ref[0, 1:2, :] += jnp.sum(row_ref[rows, :] * turn, axis=0, keepdims=True)
        return carry

    lax.fori_loop(0, tokens // step, finish, 0)


def attend_back(level, qkv, mixed_grad, wide, lse, cosine, sine, column, row_pos, pairs, first, last, into=()):
    tokens = qkv.shape[0]
    own = pair_spec(tokens, first)
    pair_rows = pl.BlockSpec((1, 2, tokens), lambda p, *_: (first + p, 0, 0))
    freqs = pl.BlockSpec((1, 2, LANES), lambda p, *_: (first + p, 0, 0))
    fixed = fixed_spec(tokens, LANES)
    out = shape(tokens, pairs * LANES, bf16)
    return call(
        attend_back_kernel,
        (last - first,),
        [own, pair_spec(tokens, pairs + first), pair_spec(tokens, 2 * pairs + first)]
        + [own, own, pair_rows, own, own, fixed, fixed]
        + [pl.BlockSpec(memory_space=pl.ANY)] * len(into),
        [own, own, own, freqs],
        (out, out, out, jax.ShapeDtypeStruct((pairs, 2, LANES), f32)),
        7e9 * (last - first),
        5 * MIB * (last - first),
        24,
        [pltpu.VMEM((tokens, LANES), f32)] * 3 + [pltpu.VMEM((8, tokens), f32)],
        1,
        2e6 * (last - first),
        {11 + k: k for k in range(len(into))},
    )(level, qkv, qkv, qkv, mixed_grad, wide, lse, cosine, sine, column, row_pos, *into)


def norm_rows(values):
    center = values - jnp.mean(values, axis=-1, keepdims=True)
    scale = lax.rsqrt(jnp.mean(center * center, axis=-1, keepdims=True) + norm_epsilon)
    return center * scale, scale


def norm_rows_back(grad, unit, scale, gain):
    scaled = grad * gain
    return scale * (
        scaled
        - jnp.mean(scaled, axis=-1, keepdims=True)
        - unit * jnp.mean(scaled * unit, axis=-1, keepdims=True)
    )


def widen(tokens_in, mine, theirs, gains, weights):
    tokens, feats = tokens_in.shape
    hid = weights.shape[1]
    block = 256

    def kernel(x_ref, mine_ref, theirs_ref, gains_ref, w_ref, hidden_ref, low_ref, z_ref, slope_ref):
        hidden = x_ref[...].astype(f32) + (mine_ref[...].astype(f32) + theirs_ref[...].astype(f32))
        hidden_ref[...] = hidden
        unit, _ = norm_rows(hidden)
        low = (unit * gains_ref[2:3, :] + gains_ref[3:4, :]).astype(bf16)
        low_ref[...] = low
        step = 512
        for at in range(0, hid, step):
            u = dot(low, w_ref[:, at : at + step], NN)
            below = 0.5 * (1.0 + lax.erf(u * (0.5**0.5)))
            z_ref[:, at : at + step] = (u * below).astype(bf16)
            slope = below + u * jnp.exp(-0.5 * u * u) * 0.3989422804014327
            slope_ref[:, at : at + step] = slope.astype(bf16)

    own = rows_spec(block, feats)
    return call(
        kernel,
        (tokens // block,),
        [own, own, own, fixed_spec(4, feats), fixed_spec(feats, hid)],
        [own, own, rows_spec(block, hid), rows_spec(block, hid)],
        (shape(tokens, feats, f32), shape(tokens, feats, bf16), shape(tokens, hid, bf16), shape(tokens, hid, bf16)),
        2 * tokens * feats * hid,
        24 * MIB,
        14,
        exps=5e6,
    )(tokens_in, mine, theirs, gains, weights)


def narrow(upstream, slope, reduce_w, expand_w):
    tokens, feats = upstream.shape
    hid = slope.shape[1]
    block = 256

    def kernel(up_ref, slope_ref, rw_ref, ew_ref, du_ref, db_ref):
        du = (dot(up_ref[...], rw_ref[...], NN) * slope_ref[...].astype(f32)).astype(bf16)
        du_ref[...] = du
        db_ref[...] = dot(du, ew_ref[...], NT).astype(bf16)

    own, wide = rows_spec(block, feats), rows_spec(block, hid)
    fixed = fixed_spec(feats, hid)
    return call(
        kernel,
        (tokens // block,),
        [own, wide, fixed, fixed],
        [wide, own],
        (shape(tokens, hid, bf16), shape(tokens, feats, bf16)),
        4 * tokens * feats * hid,
        20 * MIB,
        12,
    )(upstream, slope, reduce_w, expand_w)


def times_columns(left, right, width, at):
    tokens, feats = left.shape[0], right.shape[0]
    block = 512

    def kernel(l_ref, r_ref, out):
        out[...] = dot(l_ref[...], r_ref[...], NT).astype(bf16)

    return call(
        kernel,
        (tokens // block,),
        [rows_spec(block, width), fixed_spec(feats, width, at)],
        rows_spec(block, feats),
        shape(tokens, feats, bf16),
        2 * tokens * feats * width,
        9 * MIB,
        12,
    )(left, right)


def second_back(upstream, mine, theirs, hidden, mlp_mine, mlp_theirs, gains, weights, width, at):
    tokens, feats = upstream.shape
    block = 256

    def kernel(
        up_ref, mine_ref, theirs_ref, hidden_ref, out_mine_ref, out_theirs_ref, gains_ref, w_ref,
        act_ref, low_ref, do_ref, sums_ref,
    ):
        hidden = hidden_ref[...]
        act = hidden + (out_mine_ref[...].astype(f32) + out_theirs_ref[...].astype(f32))
        act_ref[...] = act.astype(bf16)
        grad = mine_ref[...].astype(f32) + theirs_ref[...].astype(f32)
        unit, scale = norm_rows(hidden)
        total = up_ref[...].astype(f32) + norm_rows_back(grad, unit, scale, gains_ref[2:3, :])
        low = total.astype(bf16)
        low_ref[...] = low
        do_ref[...] = dot(low, w_ref[...], NN).astype(bf16)

        @pl.when(pl.program_id(0) == 0)
        def _():
            sums_ref[...] = jnp.zeros_like(sums_ref)

        sums_ref[0:1, :] += jnp.sum(grad * unit, axis=0, keepdims=True)
        sums_ref[1:2, :] += jnp.sum(grad, axis=0, keepdims=True)

    own = rows_spec(block, feats)
    return call(
        kernel,
        (tokens // block,),
        [own] * 6 + [fixed_spec(4, feats), fixed_spec(feats, width, at)],
        [own, own, rows_spec(block, width), fixed_spec(2, feats)],
        (shape(tokens, feats, bf16), shape(tokens, feats, bf16), shape(tokens, width, bf16), shape(2, feats, f32)),
        2 * tokens * feats * width,
        24 * MIB,
        16,
    )(upstream, mine, theirs, hidden, mlp_mine, mlp_theirs, gains, weights)


def first_share(dq, dk, dv, weights):
    tokens, width = dq.shape
    feats = weights.shape[0]
    block = 256

    def kernel(dq_ref, dk_ref, dv_ref, w_ref, out):
        total = dot(dq_ref[...], w_ref[:, :width], NT)
        total = total + dot(dk_ref[...], w_ref[:, width : 2 * width], NT)
        out[...] = (total + dot(dv_ref[...], w_ref[:, 2 * width :], NT)).astype(bf16)

    own = rows_spec(block, width)
    return call(
        kernel,
        (tokens // block,),
        [own, own, own, fixed_spec(feats, 3 * width)],
        rows_spec(block, feats),
        shape(tokens, feats, bf16),
        6 * tokens * feats * width,
        8 * MIB,
        12,
    )(dq, dk, dv, weights)


def first_back(tokens_in, mine, theirs, hidden_grad, gains):
    tokens, feats = tokens_in.shape
    block = 256

    def kernel(x_ref, mine_ref, theirs_ref, hidden_ref, gains_ref, grad_ref, sums_ref):
        grad = mine_ref[...].astype(f32) + theirs_ref[...].astype(f32)
        unit, scale = norm_rows(x_ref[...].astype(f32))
        grad_ref[...] = hidden_ref[...].astype(f32) + norm_rows_back(grad, unit, scale, gains_ref[0:1, :])

        @pl.when(pl.program_id(0) == 0)
        def _():
            sums_ref[...] = jnp.zeros_like(sums_ref)

        sums_ref[0:1, :] += jnp.sum(grad * unit, axis=0, keepdims=True)
        sums_ref[1:2, :] += jnp.sum(grad, axis=0, keepdims=True)

    own = rows_spec(block, feats)
    return call(
        kernel,
        (tokens // block,),
        [own, own, own, own, fixed_spec(4, feats)],
        [own, fixed_spec(2, feats)],
        (shape(tokens, feats, f32), shape(2, feats, f32)),
        20 * tokens * feats,
        20 * MIB,
        12,
    )(tokens_in, mine, theirs, hidden_grad, gains)


def slab_layout(resolution):
    places = jnp.arange(TOK_DEV, dtype=jnp.int32)
    side_len = jnp.where(
        resolution == 0, SIDES[0], jnp.where(resolution == 1, SIDES[1], SIDES[2])
    ).astype(jnp.int32)
    patches = side_len * side_len
    image_id = places // patches
    within = places % patches
    column = (within % side_len).astype(f32)
    row_pos = (within // side_len).astype(f32)
    usable = (image_id < TOK_DEV // patches).astype(f32)
    return (column, row_pos, usable)


def norm_forward(values, gain_vec, shift_vec):
    center = values - jnp.mean(values, axis=-1, keepdims=True)
    spread = jnp.mean(center * center, axis=-1, keepdims=True)
    scale_rows = lax.rsqrt(spread + norm_epsilon)
    unit_rows = center * scale_rows
    return (unit_rows * gain_vec + shift_vec, unit_rows, scale_rows)


def adamw(weight, first, second, gradient, rate, decay):
    first = beta_first * first + (1.0 - beta_first) * gradient
    second = beta_second * second + (1.0 - beta_second) * gradient * gradient
    first_fix = 1.0 - beta_first**STEP
    second_fix = 1.0 - beta_second**STEP
    update = first / first_fix / (jnp.sqrt(second / second_fix) + adam_epsilon)
    return (first, second, weight - rate * (update + decay * weight))


def step_kernel(mp_ref, *refs):
    states, grads, sums = refs[:18], refs[18:22], refs[22]
    clip_ref, outs = refs[23], refs[24:]
    norm_grad, turned = sums[0:4, :], sums[4:6, :]
    width = turned.shape[1] // 2
    half = HD // 2
    rope = turned - pltpu.roll(turned, 2 * width - half, 1)
    lane = lax.broadcasted_iota(jnp.int32, turned.shape, 1)
    rope = jnp.where(lane % HD < half, rope, 0.0)
    total = sums[6:7, 0:1] + jnp.sum(
        jnp.sum(norm_grad * norm_grad, axis=0, keepdims=True) + jnp.sum(rope * rope, axis=0, keepdims=True),
        axis=1,
        keepdims=True,
    )
    clip = jnp.sqrt(total)
    clip_ref[...] = clip
    factor = jnp.minimum(1.0, clip_limit / clip)
    for p in range(4):
        weight, first, second = states[3 * p : 3 * p + 3]
        results = outs[3 * p : 3 * p + 3]
        if p == 0:
            cols = weight.shape[2]
            for k in range(weight.shape[0]):
                grad = grads[0][:, k * cols : (k + 1) * cols] * factor
                new = adamw(weight[k], first[k], second[k], grad, matrix_rate, matrix_decay)
                for out, value in zip(results, new):
                    out[k] = value
            continue
        new = adamw(weight[...], first[...], second[...], grads[p][...] * factor, matrix_rate, matrix_decay)
        for out, value in zip(results, new):
            out[...] = value
    weight, first, second = states[12:15]
    for out, value in zip(outs[12:15], adamw(weight[...], first[...], second[...], norm_grad * factor, vector_rate, 0.0)):
        out[...] = value
    own = jnp.where(mp_ref[0] == 0, rope[:, :width], rope[:, width:]) * factor
    weight, first, second = states[15:18]
    for h in range(weight.shape[0]):
        grad = own[:, h * HD : h * HD + half]
        for out, value in zip(outs[15:18], adamw(weight[h], first[h], second[h], grad, vector_rate, 0.0)):
            out[h] = value


def optimize(core, states, grads, sums):
    outs = tuple(jax.ShapeDtypeStruct(a.shape, f32) for a in states)
    small = tuple(pltpu.with_memory_space_constraint(a, pltpu.HBM) for a in states[12:])
    args = states[:12] + small + grads + (sums,)
    return pl.pallas_call(
        step_kernel,
        out_shape=(jax.ShapeDtypeStruct((1, 1), f32),) + outs,
        grid_spec=pltpu.PrefetchScalarGridSpec(num_scalar_prefetch=1, grid=()),
        compiler_params=pltpu.CompilerParams(vmem_limit_bytes=16 * MIB),
        name="optimize",
    )(core, *args)


def local(
    size,
    tokens,
    cotangent,
    device_class,
    input_proj,
    output_proj,
    expand_proj,
    reduce_proj,
    norm_params,
    rope_freqs,
    input_first,
    input_second,
    output_first,
    output_second,
    expand_first,
    expand_second,
    reduce_first,
    reduce_second,
    norm_first,
    norm_second,
    rope_first,
    rope_second,
):
    heads = rope_freqs.shape[1]
    width = heads * HD
    pairs = width // LANES
    me = lax.axis_index("dp").astype(jnp.int32)
    rows = input_proj.shape[0]

    attn_shard = jnp.concatenate(
        [input_proj.reshape(rows, 3 * width).astype(bf16), output_proj.astype(bf16)], axis=1
    )
    attn_far = gather_far(attn_shard, size)
    attn_pieces = gather_near(attn_far, size)
    expand_far = gather_far(tie(expand_proj.astype(bf16), attn_far), size)
    expand_pieces = gather_near(tie(expand_far, *attn_pieces[0], *attn_pieces[1]), size)
    reduce_far = gather_far(tie(reduce_proj.astype(bf16), expand_far), size)
    reduce_pieces = gather_near(tie(reduce_far, *expand_pieces[0], *expand_pieces[1]), size)

    column, row_pos, usable = slab_layout(device_class[0])
    gains = norm_params.T
    normed = norm_forward(tokens.astype(f32), norm_params[:, 0], norm_params[:, 1])[0].astype(bf16)
    half = HD // 2
    freqs = jnp.concatenate([rope_freqs, rope_freqs], axis=2).reshape(2, width)
    angles = column[:, None] * freqs[0][None] + row_pos[:, None] * freqs[1][None]
    cosine = jnp.cos(angles)
    sine = jnp.sin(angles) * jnp.where(jnp.arange(width) % HD < half, -1.0, 1.0)[None]
    column = jnp.broadcast_to(column[:, None], (TOK_DEV, LANES))
    row_pos = jnp.broadcast_to(row_pos[:, None], (TOK_DEV, LANES))
    upstream = (cotangent.astype(f32) * usable[:, None]).astype(bf16)

    def product(terms, color, *place):
        return grad_halves(terms, orders(size)[color], size, me, *place)

    attn_whole = whole(attn_pieces, size, me)
    qkv = project(normed, attn_whole, cosine, sine, width)
    mixed, mixed_wide, lse = attend(device_class, qkv, pairs)
    attn_part = times_columns(mixed, attn_whole, width, 3)
    attn_other = traded(attn_part)
    whole_expand = whole(expand_pieces, size, me)
    hidden_rows, second_in, activ, slope = widen(tokens, attn_part, attn_other, gains, whole_expand)
    wide = activ.shape[1] // 2
    reduce_halves = [product([(upstream, activ, c, wide)], c) for c in range(2)]
    reduce_shard = scatter(reduce_halves, size)
    whole_reduce = whole(reduce_pieces, size, me)
    mlp_part = times_columns(activ, whole_reduce, 2 * wide, 0)
    mlp_other = traded(mlp_part)
    expanded_low, second_part = narrow(upstream, slope, whole_reduce, whole_expand)
    second_other = traded(second_part)
    lead = width - LANES
    cuts = (wide + lead, wide + LANES)
    expand_halves = [product([(second_in, expanded_low, c, wide)], c, cuts[c]) for c in range(2)]
    activations, attn_low, mixed_low, sums_two = second_back(
        upstream, second_part, second_other, hidden_rows, mlp_part, mlp_other, gains, attn_whole, width, 3
    )
    expand_halves = [
        product([(attn_low, mixed, 0, lead)], 0, cuts[0], wide, expand_halves[0]),
        product([(attn_low, mixed, lead // LANES, LANES)], 1, cuts[1], wide, expand_halves[1]),
    ]
    both = scatter(expand_halves, size)
    expand_shard = jnp.concatenate([both[:, :wide], both[:, cuts[0] : cuts[0] + wide]], axis=1)
    output_shard = jnp.concatenate([both[:, wide : cuts[0]], both[:, cuts[0] + wide :]], axis=1)
    back = (device_class, qkv, mixed_low, mixed_wide, lse, cosine, sine, column, row_pos, pairs)
    done = attend_back(*back, 0, pairs - 1)
    dq, dk, dv, turn = attend_back(*back, pairs - 1, pairs, done)
    turn = turn.transpose(1, 0, 2).reshape(2, width)
    turn_other = traded(turn)
    core = lax.axis_index("mp").astype(jnp.int32)
    turns = jnp.where(
        core == 0, jnp.concatenate([turn, turn_other], axis=1), jnp.concatenate([turn_other, turn], axis=1)
    )
    input_halves = [
        product([(normed, dq, 0, width), (normed, dk, 0, lead)], 0),
        product([(normed, dk, lead // LANES, LANES), (normed, dv, 0, width)], 1),
    ]
    input_shard = scatter(input_halves, size)
    first_part = first_share(dq, dk, dv, attn_whole)
    first_other = traded(first_part)
    input_grad, sums_one = first_back(tokens, first_part, first_other, attn_low, gains)

    partial_squares = (
        jnp.sum(input_shard * input_shard)
        + jnp.sum(output_shard * output_shard)
        + jnp.sum(expand_shard * expand_shard)
        + jnp.sum(reduce_shard * reduce_shard)
    )
    squares = partial_squares + lax.ppermute(partial_squares, "mp", [(0, 1), (1, 0)])
    feats = tokens.shape[1]
    vectors = jnp.concatenate([sums_one, sums_two, turns, jnp.zeros((2, feats), f32)], axis=0)
    sums = butterfly(jnp.where(jnp.arange(8)[:, None] == 6, squares, vectors), size)

    def flip(value):
        return value.transpose(1, 0, 2)

    states = (
        tuple(flip(a) for a in (input_proj, input_first, input_second))
        + (output_proj, output_first, output_second)
        + (expand_proj, expand_first, expand_second)
        + (reduce_proj, reduce_first, reduce_second)
        + (norm_params.T, norm_first.T, norm_second.T)
        + tuple(flip(a) for a in (rope_freqs, rope_first, rope_second))
    )
    grads = (input_shard, output_shard, expand_shard, reduce_shard)
    clip_norm, *new = optimize(core[None], states, grads, sums)
    new = (
        [flip(a) for a in new[:3]]
        + new[3:12]
        + [a.T for a in new[12:15]]
        + [flip(a) for a in new[15:]]
    )
    return (activations, input_grad, clip_norm.reshape(()), *new)


def solution(mesh):
    rows, cube, flat, full = P("dp", None), P("dp", None, "mp"), P("dp", "mp"), P()
    rope = P(None, "mp", None)
    in_specs = (
        (rows, rows, P("dp"), cube, flat, flat, flat, full, rope)
        + (cube, cube)
        + (flat,) * 6
        + (full, full, rope, rope)
    )
    out_specs = (rows, rows, full) + (cube,) * 3 + (flat,) * 9 + (full,) * 3 + (rope,) * 3

    def step(*args):
        return local(mesh.shape["dp"], *args)

    step = jax.shard_map(step, mesh=mesh, in_specs=in_specs, out_specs=out_specs, check_vma=False)
    return step
```

```python
import jax
import jax.numpy as jnp
from jax import lax
from jax.experimental import pallas as pl
from jax.experimental.pallas import tpu as pltpu
from jax.sharding import PartitionSpec as P


HD = 64
SIDES = (14, 20, 24)
STEP = 10
TOK_DEV = 1536

norm_epsilon = 1e-06
adam_epsilon = 1e-08
beta_first = 0.9
beta_second = 0.999
clip_limit = 1.0
matrix_rate = 0.05
matrix_decay = 0.05
vector_rate = 0.5

bf16 = jnp.bfloat16
f32 = jnp.float32
NT = (((1,), (1,)), ((), ()))
NN = (((1,), (0,)), ((), ()))
TN = (((0,), (0,)), ((), ()))
LANES = 128
MIB = 1024 * 1024


def dot(a, b, dims):
    return lax.dot_general(a, b, dims, preferred_element_type=f32)


def swap(value, axis, size, bit):
    return lax.ppermute(value, axis, [(i, i ^ bit) for i in range(size)])


def bits_of(size):
    return [1 << b for b in reversed(range(size.bit_length() - 1))]


def orders(size):
    bits = bits_of(size)
    return (bits, bits[:-2] + [bits[-1], bits[-2]])


def masks_of(order):
    masks = [0]
    for bit in order:
        masks = masks + [m ^ bit for m in masks]
    return masks


def tie(value, *others):
    return lax.optimization_barrier((value,) + others)[0]


def gather_far(shard, size):
    cur = shard[None]
    for bit in bits_of(size)[:-2]:
        cur = jnp.concatenate([cur, swap(cur, "dp", size, bit)], axis=0)
    return cur


def gather_near(cur, size, cut):
    parts = [cur[:, :, :cut], cur[:, :, cut:]]
    for color, order in enumerate(orders(size)):
        parts[color] = jnp.concatenate(
            [parts[color], swap(parts[color], "dp", size, order[-2])], axis=0
        )
    out = []
    for color, order in enumerate(orders(size)):
        out.append((parts[color], swap(parts[color], "dp", size, order[-1])))
    return out


def whole(pieces, size, me):
    rows = pieces[0][0].shape[1]
    widths = [low.shape[2] for low, _ in pieces]
    masks = [masks_of(order) for order in orders(size)]
    if rows % 16:
        cols = []
        for (low, high), ms, width in zip(pieces, masks, widths):
            place = [0] * size
            for at, m in enumerate(ms):
                place[m] = at
            both = jnp.concatenate([low, high], axis=0)
            index = jnp.array(place, jnp.int32)[jnp.arange(size, dtype=jnp.int32) ^ me]
            cols.append(jnp.take(both, index, axis=0).reshape(size * rows, width))
        return jnp.concatenate(cols, axis=1)

    def kernel(me_ref, a0, a1, b0, b1, out):
        own = me_ref[0]
        col = 0
        for color, pair in enumerate(((a0, a1), (b0, b1))):
            for j, mask in enumerate(masks[color]):
                src = pair[j // (size // 2)]
                at = pl.multiple_of((own ^ mask) * rows, 16)
                out[pl.ds(at, rows), col : col + widths[color]] = src[j % (size // 2)]
            col += widths[color]

    flat = [p for pair in pieces for p in pair]
    return pl.pallas_call(
        kernel,
        out_shape=jax.ShapeDtypeStruct((size * rows, sum(widths)), bf16),
        grid_spec=pltpu.PrefetchScalarGridSpec(
            num_scalar_prefetch=1,
            grid=(1,),
            in_specs=[pl.BlockSpec(p.shape, lambda i, c: (0, 0, 0)) for p in flat],
            out_specs=pl.BlockSpec((size * rows, sum(widths)), lambda i, c: (0, 0)),
        ),
        compiler_params=pltpu.CompilerParams(vmem_limit_bytes=12 * MIB),
        name="whole",
    )(me[None], *flat)


def grad_halves(terms, order, size, me, total=None, at=0, into=()):
    ms = masks_of(order)
    count = size // 2
    feats = terms[0][0].shape[1]
    rows = feats // size
    width = sum(w for _, _, _, w in terms)
    total = total or width
    if rows % 16:
        mat = jnp.concatenate(
            [dot(l, r[:, c * w : (c + 1) * w], TN) for l, r, c, w in terms], axis=1
        ).reshape(size, rows, width)
        mat = jnp.take(mat, jnp.array(ms, jnp.int32) ^ me, axis=0)
        halves = (mat[:count], mat[count:].astype(bf16))
        return tuple(jnp.concatenate([a, b], axis=2) for a, b in zip(into, halves)) if into else halves

    def kernel(me_ref, *refs):
        ins, (keep, send, acc) = refs[: 2 * len(terms)], refs[2 * len(terms) + len(into) :]
        own = me_ref[0]
        col = 0
        for t, (_, _, _, w) in enumerate(terms):
            acc[:, col : col + w] = dot(ins[2 * t][...], ins[2 * t + 1][...], TN)
            col += w
        for j, mask in enumerate(ms):
            block = acc[pl.ds(pl.multiple_of((own ^ mask) * rows, 16), rows), :]
            if j < count:
                keep[j] = block
            else:
                send[j - count] = block.astype(bf16)

    in_specs, args = [], []
    for l, r, c, w in terms:
        in_specs.append(pl.BlockSpec(l.shape, lambda i, m: (0, 0)))
        in_specs.append(pl.BlockSpec((r.shape[0], w), lambda i, m, c=c: (0, c)))
        args += [l, r]
    aliases = {1 + len(args) + k: k for k in range(len(into))}
    in_specs += [pl.BlockSpec(memory_space=pl.ANY)] * len(into)
    flops = sum(2 * l.shape[0] * l.shape[1] * w for l, _, _, w in terms)
    return pl.pallas_call(
        kernel,
        out_shape=(
            jax.ShapeDtypeStruct((count, rows, total), f32),
            jax.ShapeDtypeStruct((count, rows, total), bf16),
        ),
        grid_spec=pltpu.PrefetchScalarGridSpec(
            num_scalar_prefetch=1,
            grid=(1,),
            in_specs=in_specs,
            out_specs=[pl.BlockSpec((count, rows, width), lambda i, m: (0, 0, at // width))] * 2,
            scratch_shapes=[pltpu.VMEM((feats, width), f32)],
        ),
        input_output_aliases=aliases,
        compiler_params=pltpu.CompilerParams(vmem_limit_bytes=18 * MIB),
        cost_estimate=pl.CostEstimate(flops=flops, transcendentals=0, bytes_accessed=12 * MIB),
        name="grad_halves",
    )(me[None], *args, *into)


def joined(keep, got):
    count = keep.shape[0] // 2
    kept = keep[:count] + got[:count].astype(f32)
    return kept, (keep[count:] + got[count:].astype(f32)).astype(bf16)


def scatter(halves, size):
    halves = list(halves)
    for color, order in enumerate(orders(size)):
        keep, send = halves[color]
        halves[color] = joined(keep, swap(send, "dp", size, order[-1]))
    for color, order in enumerate(orders(size)):
        keep, send = halves[color]
        halves[color] = joined(keep, swap(send, "dp", size, order[-2]))
    keep, send = (jnp.concatenate([halves[0][k], halves[1][k]], axis=2) for k in range(2))
    far = bits_of(size)[:-2][::-1]
    for bit in far[:-1]:
        keep, send = joined(keep, swap(send, "dp", size, bit))
    got = swap(send, "dp", size, far[-1])
    return keep, got, send


def added(keep, got):
    total = keep + got.astype(f32)
    return total.reshape(total.shape[1:])


def traded(part):
    return lax.ppermute(part, "mp", [(0, 1), (1, 0)])


def butterfly(value, size):
    bits = bits_of(size)[::-1]
    for bit in bits[:-1]:
        value = value + swap(value, "dp", size, bit)
    return value, swap(value, "dp", size, bits[-1])


def call(kernel, grid, in_specs, out_specs, out_shape, flops, bytes_accessed, vmem, scratch=(), prefetch=0, exps=0, aliases=None):
    return pl.pallas_call(
        kernel,
        out_shape=out_shape,
        grid_spec=pltpu.PrefetchScalarGridSpec(
            num_scalar_prefetch=prefetch,
            grid=grid,
            in_specs=in_specs,
            out_specs=out_specs,
            scratch_shapes=scratch,
        ),
        input_output_aliases=aliases or {},
        compiler_params=pltpu.CompilerParams(vmem_limit_bytes=vmem * MIB),
        cost_estimate=pl.CostEstimate(
            flops=int(flops), transcendentals=int(exps), bytes_accessed=int(bytes_accessed)
        ),
    )


def shape(rows, cols, kind):
    return jax.ShapeDtypeStruct((rows, cols), kind)


def rows_spec(block, cols, at=0):
    return pl.BlockSpec((block, cols), lambda i, *_: (i, at))


def fixed_spec(rows, cols, at=0):
    return pl.BlockSpec((rows, cols), lambda i, *_: (0, at))


def partner(values):
    half, width = HD // 2, values.shape[1]
    lane = lax.broadcasted_iota(jnp.int32, (1, width), 1)
    return jnp.where(lane % HD < half, pltpu.roll(values, width - half, 1), pltpu.roll(values, half, 1))


def project(normed, weights, cosine, sine, width):
    tokens, feats = normed.shape
    block = 256

    def kernel(a_ref, w_ref, cos_ref, sin_ref, out):
        joined = dot(a_ref[...], w_ref[...], NN)
        cos, sin = cos_ref[...], sin_ref[...]
        query, key = joined[:, :width], joined[:, width : 2 * width]
        query = query * cos + partner(query) * sin
        out[:, :width] = (query * 0.125).astype(bf16)
        out[:, width : 2 * width] = (key * cos + partner(key) * sin).astype(bf16)
        out[:, 2 * width :] = joined[:, 2 * width :].astype(bf16)

    return call(
        kernel,
        (tokens // block,),
        [rows_spec(block, feats), fixed_spec(feats, 3 * width), rows_spec(block, width), rows_spec(block, width)],
        rows_spec(block, 3 * width),
        shape(tokens, 3 * width, bf16),
        6 * tokens * feats * width,
        13 * MIB,
        14,
    )(normed, weights, cosine, sine)


def images(level):
    patches = SIDES[level] ** 2
    out = []
    for i in range(-(-TOK_DEV // patches)):
        first, last = i * patches, min((i + 1) * patches, TOK_DEV)
        at, end = first // 16 * 16, -(-last // 16) * 16
        out.append((at, end - at, first - at, last - at))
    return out


def heads_of(block):
    lane = lax.broadcasted_iota(jnp.int32, block.shape, 1)
    zero = jnp.zeros_like(block)
    return jnp.where(lane < HD, block, zero), jnp.where(lane < HD, zero, block)


def attend_kernel(level_ref, q_ref, k_ref, v_ref, o_ref, wide_ref, lse_ref, stat_ref):
    def image(at, window, lo, hi):
        masked = lo != 0 or hi != window
        rows = pl.ds(at, window)
        keys, values = k_ref[rows, :], v_ref[rows, :]
        mixes, stats = [], []
        heads = heads_of(q_ref[rows, :])
        ahead = [dot(head, keys, NT) for head in heads] if window > 512 else None
        for h, head in enumerate(heads):
            scores = ahead[h] if ahead else dot(head, keys, NT)
            if masked:
                place = lax.broadcasted_iota(jnp.int32, scores.shape, 1)
                scores = jnp.where((place >= lo) & (place < hi), scores, -1e30)
            peak = jnp.max(scores, axis=-1, keepdims=True)
            expo = jnp.exp(scores - peak)
            total = jnp.sum(expo, axis=-1, keepdims=True)
            mixes.append(dot(expo.astype(bf16), values, NN) / total)
            stats.append(peak + jnp.log(total))
        lane = lax.broadcasted_iota(jnp.int32, mixes[0].shape, 1)
        mix = jnp.where(lane < HD, mixes[0], mixes[1])
        stat = jnp.where(lane < HD, stats[0], stats[1])
        if masked:
            place = lax.broadcasted_iota(jnp.int32, mix.shape, 0)
            own = (place >= lo) & (place < hi)
            mix = jnp.where(own, mix, wide_ref[rows, :])
            stat = jnp.where(own, stat, stat_ref[rows, :])
        wide_ref[rows, :] = mix
        stat_ref[rows, :] = stat

    for level in range(3):

        @pl.when(level_ref[0] == level)
        def _(level=level):
            for one in images(level):
                image(*one)

    o_ref[...] = wide_ref[...].astype(bf16)
    turned = stat_ref[...].T
    lse_ref[0, 0:1, :] = turned[0:1]
    lse_ref[0, 1:2, :] = turned[HD : HD + 1]


def pair_spec(tokens, at):
    return pl.BlockSpec((tokens, LANES), lambda p, *_: (0, at + p))


def attend(level, qkv, pairs):
    tokens = qkv.shape[0]
    stats = pl.BlockSpec((1, 2, tokens), lambda p, *_: (p, 0, 0))
    return call(
        attend_kernel,
        (pairs,),
        [pair_spec(tokens, 0), pair_spec(tokens, pairs), pair_spec(tokens, 2 * pairs)],
        [pair_spec(tokens, 0), pair_spec(tokens, 0), stats],
        (
            shape(tokens, pairs * LANES, bf16),
            shape(tokens, pairs * LANES, f32),
            jax.ShapeDtypeStruct((pairs, 2, tokens), f32),
        ),
        8e9,
        9 * MIB,
        18,
        [pltpu.VMEM((tokens, LANES), f32)],
        1,
        5e6,
    )(level, qkv, qkv, qkv)


def attend_back_kernel(
    level_ref, q_ref, k_ref, v_ref, do_ref, wide_ref, lse_ref, cos_ref, sin_ref, col_ref, row_ref, *refs
):
    dq_ref, dk_ref, dv_ref, freq_ref, dq_acc, dk_acc, dv_acc, inner_ref = refs[-8:]
    tokens = q_ref.shape[0]
    lane = lax.broadcasted_iota(jnp.int32, (8, LANES), 1)
    line = lax.broadcasted_iota(jnp.int32, (8, LANES), 0)
    pick = jnp.where(lane // HD == line, 1.0, 0.0).astype(f32)
    step = 256
    for at in range(0, tokens, step):
        inner_ref[:, at : at + step] = lax.dot_general(
            pick,
            do_ref[at : at + step, :].astype(f32) * wide_ref[at : at + step, :],
            NT,
            precision=lax.Precision.HIGHEST,
            preferred_element_type=f32,
        )

    def lanes_from(values, at, window):
        return (pltpu.roll(values, tokens - at, 1) if at else values)[:, :window]

    def image(at, window, lo, hi):
        masked = lo != 0 or hi != window
        rows = pl.ds(at, window)
        queries, grads = heads_of(q_ref[rows, :]), heads_of(do_ref[rows, :])
        keys, values = k_ref[rows, :], v_ref[rows, :]
        lse, inner = lanes_from(lse_ref[0], at, window), lanes_from(inner_ref[...], at, window)
        dq, dk, dv = [], [], []
        scores = [dot(keys, query, NT) for query in queries]
        prob_grads = [dot(values, grad, NT) for grad in grads]
        for h, key in enumerate(heads_of(keys)):
            probs = jnp.exp(scores[h] - lse[h : h + 1])
            if masked:
                place = lax.broadcasted_iota(jnp.int32, probs.shape, 0)
                asked = lax.broadcasted_iota(jnp.int32, probs.shape, 1)
                own = (place >= lo) & (place < hi) & (asked >= lo) & (asked < hi)
                probs = jnp.where(own, probs, 0.0)
            low = (probs * (prob_grads[h] - inner[h : h + 1])).astype(bf16)
            dv.append(dot(probs.astype(bf16), grads[h], NN))
            dk.append(dot(low, queries[h], NN))
            dq.append(dot(key, low, TN))
        for acc, total in ((dq_acc, (dq[0] + dq[1]).T), (dk_acc, dk[0] + dk[1]), (dv_acc, dv[0] + dv[1])):
            acc[rows, :] = acc[rows, :] + total if masked else total

    for level in range(3):

        @pl.when(level_ref[0] == level)
        def _(level=level):
            if any(lo != 0 or hi != window for _, window, lo, hi in images(level)):
                for acc in (dq_acc, dk_acc, dv_acc):
                    acc[...] = jnp.zeros_like(acc)
            for one in images(level):
                image(*one)

    freq_ref[...] = jnp.zeros_like(freq_ref)

    def finish(c, carry):
        rows = pl.ds(pl.multiple_of(c * step, step), step)
        cosine, sine = cos_ref[rows, :], sin_ref[rows, :]
        dq, dk = dq_acc[rows, :] * 0.125, dk_acc[rows, :]
        dq_other, dk_other = partner(dq), partner(dk)
        dq_ref[rows, :] = (dq * cosine - dq_other * sine).astype(bf16)
        dk_ref[rows, :] = (dk * cosine - dk_other * sine).astype(bf16)
        dv_ref[rows, :] = dv_acc[rows, :].astype(bf16)
        turn = q_ref[rows, :].astype(f32) * 8.0 * dq_other + k_ref[rows, :].astype(f32) * dk_other
        freq_ref[0, 0:1, :] += jnp.sum(col_ref[rows, :] * turn, axis=0, keepdims=True)
        freq_ref[0, 1:2, :] += jnp.sum(row_ref[rows, :] * turn, axis=0, keepdims=True)
        return carry

    lax.fori_loop(0, tokens // step, finish, 0)


def attend_back(level, qkv, mixed_grad, wide, lse, cosine, sine, column, row_pos, pairs, first, last, into=()):
    tokens = qkv.shape[0]
    own = pair_spec(tokens, first)
    pair_rows = pl.BlockSpec((1, 2, tokens), lambda p, *_: (first + p, 0, 0))
    freqs = pl.BlockSpec((1, 2, LANES), lambda p, *_: (first + p, 0, 0))
    fixed = fixed_spec(tokens, LANES)
    out = shape(tokens, pairs * LANES, bf16)
    return call(
        attend_back_kernel,
        (last - first,),
        [own, pair_spec(tokens, pairs + first), pair_spec(tokens, 2 * pairs + first)]
        + [own, own, pair_rows, own, own, fixed, fixed]
        + [pl.BlockSpec(memory_space=pl.ANY)] * len(into),
        [own, own, own, freqs],
        (out, out, out, jax.ShapeDtypeStruct((pairs, 2, LANES), f32)),
        7e9 * (last - first),
        5 * MIB * (last - first),
        24,
        [pltpu.VMEM((tokens, LANES), f32)] * 3 + [pltpu.VMEM((8, tokens), f32)],
        1,
        2e6 * (last - first),
        {11 + k: k for k in range(len(into))},
    )(level, qkv, qkv, qkv, mixed_grad, wide, lse, cosine, sine, column, row_pos, *into)


def norm_rows(values):
    center = values - jnp.mean(values, axis=-1, keepdims=True)
    scale = lax.rsqrt(jnp.mean(center * center, axis=-1, keepdims=True) + norm_epsilon)
    return center * scale, scale


def norm_rows_back(grad, unit, scale, gain):
    scaled = grad * gain
    return scale * (
        scaled
        - jnp.mean(scaled, axis=-1, keepdims=True)
        - unit * jnp.mean(scaled * unit, axis=-1, keepdims=True)
    )


def widen(tokens_in, mine, theirs, gains, weights, hid):
    tokens, feats = tokens_in.shape
    block = 256

    def kernel(x_ref, mine_ref, theirs_ref, gains_ref, w_ref, hidden_ref, low_ref, z_ref, slope_ref):
        hidden = x_ref[...].astype(f32) + (mine_ref[...].astype(f32) + theirs_ref[...].astype(f32))
        hidden_ref[...] = hidden
        unit, _ = norm_rows(hidden)
        low = (unit * gains_ref[2:3, :] + gains_ref[3:4, :]).astype(bf16)
        low_ref[...] = low
        step = 512
        for at in range(0, hid, step):
            u = dot(low, w_ref[:, at : at + step], NN)
            below = 0.5 * (1.0 + lax.erf(u * (0.5**0.5)))
            z_ref[:, at : at + step] = (u * below).astype(bf16)
            slope = below + u * jnp.exp(-0.5 * u * u) * 0.3989422804014327
            slope_ref[:, at : at + step] = slope.astype(bf16)

    own = rows_spec(block, feats)
    return call(
        kernel,
        (tokens // block,),
        [own, own, own, fixed_spec(4, feats), fixed_spec(feats, hid)],
        [own, own, rows_spec(block, hid), rows_spec(block, hid)],
        (shape(tokens, feats, f32), shape(tokens, feats, bf16), shape(tokens, hid, bf16), shape(tokens, hid, bf16)),
        2 * tokens * feats * hid,
        24 * MIB,
        14,
        exps=5e6,
    )(tokens_in, mine, theirs, gains, weights)


def narrow(upstream, slope, reduce_w, expand_w):
    tokens, feats = upstream.shape
    hid = slope.shape[1]
    block = 256

    def kernel(up_ref, slope_ref, rw_ref, ew_ref, du_ref, db_ref):
        du = (dot(up_ref[...], rw_ref[...], NN) * slope_ref[...].astype(f32)).astype(bf16)
        du_ref[...] = du
        db_ref[...] = dot(du, ew_ref[...], NT).astype(bf16)

    own, wide = rows_spec(block, feats), rows_spec(block, hid)
    fixed = fixed_spec(feats, hid)
    return call(
        kernel,
        (tokens // block,),
        [own, wide, fixed, fixed],
        [wide, own],
        (shape(tokens, hid, bf16), shape(tokens, feats, bf16)),
        4 * tokens * feats * hid,
        20 * MIB,
        12,
    )(upstream, slope, reduce_w, expand_w)


def times_columns(left, right, width, at):
    tokens, feats = left.shape[0], right.shape[0]
    block = 512

    def kernel(l_ref, r_ref, out):
        out[...] = dot(l_ref[...], r_ref[...], NT).astype(bf16)

    return call(
        kernel,
        (tokens // block,),
        [rows_spec(block, width), fixed_spec(feats, width, at)],
        rows_spec(block, feats),
        shape(tokens, feats, bf16),
        2 * tokens * feats * width,
        9 * MIB,
        12,
    )(left, right)


def second_back(upstream, mine, theirs, hidden, mlp_mine, mlp_theirs, gains, weights, width, at):
    tokens, feats = upstream.shape
    block = 512

    def kernel(
        up_ref, mine_ref, theirs_ref, hidden_ref, out_mine_ref, out_theirs_ref, gains_ref, w_ref,
        act_ref, low_ref, do_ref, sums_ref,
    ):
        hidden = hidden_ref[...]
        act = hidden + (out_mine_ref[...].astype(f32) + out_theirs_ref[...].astype(f32))
        act_ref[...] = act.astype(bf16)
        grad = mine_ref[...].astype(f32) + theirs_ref[...].astype(f32)
        unit, scale = norm_rows(hidden)
        total = up_ref[...].astype(f32) + norm_rows_back(grad, unit, scale, gains_ref[2:3, :])
        low = total.astype(bf16)
        low_ref[...] = low
        do_ref[...] = dot(low, w_ref[...], NN).astype(bf16)

        @pl.when(pl.program_id(0) == 0)
        def _():
            sums_ref[...] = jnp.zeros_like(sums_ref)

        sums_ref[0:1, :] += jnp.sum(grad * unit, axis=0, keepdims=True)
        sums_ref[1:2, :] += jnp.sum(grad, axis=0, keepdims=True)

    own = rows_spec(block, feats)
    return call(
        kernel,
        (tokens // block,),
        [own] * 6 + [fixed_spec(4, feats), fixed_spec(feats, width, at)],
        [own, own, rows_spec(block, width), fixed_spec(2, feats)],
        (shape(tokens, feats, bf16), shape(tokens, feats, bf16), shape(tokens, width, bf16), shape(2, feats, f32)),
        2 * tokens * feats * width,
        24 * MIB,
        16,
    )(upstream, mine, theirs, hidden, mlp_mine, mlp_theirs, gains, weights)


def first_share(dq, dk, dv, weights):
    tokens, width = dq.shape
    feats = weights.shape[0]
    block = 256

    def kernel(dq_ref, dk_ref, dv_ref, w_ref, out):
        total = dot(dq_ref[...], w_ref[:, :width], NT)
        total = total + dot(dk_ref[...], w_ref[:, width : 2 * width], NT)
        out[...] = (total + dot(dv_ref[...], w_ref[:, 2 * width :], NT)).astype(bf16)

    own = rows_spec(block, width)
    return call(
        kernel,
        (tokens // block,),
        [own, own, own, fixed_spec(feats, 3 * width)],
        rows_spec(block, feats),
        shape(tokens, feats, bf16),
        6 * tokens * feats * width,
        8 * MIB,
        12,
    )(dq, dk, dv, weights)


def first_back(tokens_in, mine, theirs, hidden_grad, gains):
    tokens, feats = tokens_in.shape
    block = 512

    def kernel(x_ref, mine_ref, theirs_ref, hidden_ref, gains_ref, grad_ref, sums_ref):
        grad = mine_ref[...].astype(f32) + theirs_ref[...].astype(f32)
        unit, scale = norm_rows(x_ref[...].astype(f32))
        grad_ref[...] = hidden_ref[...].astype(f32) + norm_rows_back(grad, unit, scale, gains_ref[0:1, :])

        @pl.when(pl.program_id(0) == 0)
        def _():
            sums_ref[...] = jnp.zeros_like(sums_ref)

        sums_ref[0:1, :] += jnp.sum(grad * unit, axis=0, keepdims=True)
        sums_ref[1:2, :] += jnp.sum(grad, axis=0, keepdims=True)

    own = rows_spec(block, feats)
    return call(
        kernel,
        (tokens // block,),
        [own, own, own, own, fixed_spec(4, feats)],
        [own, fixed_spec(2, feats)],
        (shape(tokens, feats, f32), shape(2, feats, f32)),
        20 * tokens * feats,
        20 * MIB,
        20,
    )(tokens_in, mine, theirs, hidden_grad, gains)


def slab_layout(resolution):
    places = jnp.arange(TOK_DEV, dtype=jnp.int32)
    side_len = jnp.where(
        resolution == 0, SIDES[0], jnp.where(resolution == 1, SIDES[1], SIDES[2])
    ).astype(jnp.int32)
    patches = side_len * side_len
    image_id = places // patches
    within = places % patches
    column = (within % side_len).astype(f32)
    row_pos = (within // side_len).astype(f32)
    usable = (image_id < TOK_DEV // patches).astype(f32)
    return (column, row_pos, usable)


def norm_forward(values, gain_vec, shift_vec):
    center = values - jnp.mean(values, axis=-1, keepdims=True)
    spread = jnp.mean(center * center, axis=-1, keepdims=True)
    scale_rows = lax.rsqrt(spread + norm_epsilon)
    unit_rows = center * scale_rows
    return (unit_rows * gain_vec + shift_vec, unit_rows, scale_rows)


def adamw(weight, first, second, gradient, rate, decay):
    first = beta_first * first + (1.0 - beta_first) * gradient
    second = beta_second * second + (1.0 - beta_second) * gradient * gradient
    first_fix = 1.0 - beta_first**STEP
    second_fix = 1.0 - beta_second**STEP
    update = first / first_fix / (jnp.sqrt(second / second_fix) + adam_epsilon)
    return (first, second, weight - rate * (update + decay * weight))


def step_kernel(mp_ref, *refs):
    states, sums = refs[:18], refs[21][...] + refs[22][...]
    input_grad, both, reduce_grad = refs[18:21]
    clip_ref, outs = refs[23], refs[24:]
    wide, lead = states[6].shape[1] // 2, states[3].shape[1] - LANES
    split = wide + lead
    places = (
        None,
        ((wide, split, 0), (split + wide, split + wide + LANES, lead)),
        ((0, wide, 0), (split, split + wide, wide)),
    )
    norm_grad, turned = sums[0:4, :], sums[4:6, :]
    width = turned.shape[1] // 2
    half = HD // 2
    rope = turned - pltpu.roll(turned, 2 * width - half, 1)
    lane = lax.broadcasted_iota(jnp.int32, turned.shape, 1)
    rope = jnp.where(lane % HD < half, rope, 0.0)
    total = sums[6:7, 0:1] + jnp.sum(
        jnp.sum(norm_grad * norm_grad, axis=0, keepdims=True) + jnp.sum(rope * rope, axis=0, keepdims=True),
        axis=1,
        keepdims=True,
    )
    clip = jnp.sqrt(total)
    clip_ref[...] = clip
    factor = jnp.minimum(1.0, clip_limit / clip)
    for p in range(4):
        weight, first, second = states[3 * p : 3 * p + 3]
        results = outs[3 * p : 3 * p + 3]
        if p == 0:
            cols = weight.shape[2]
            for k in range(weight.shape[0]):
                grad = input_grad[:, k * cols : (k + 1) * cols] * factor
                new = adamw(weight[k], first[k], second[k], grad, matrix_rate, matrix_decay)
                for out, value in zip(results, new):
                    out[k] = value
        elif p == 3:
            new = adamw(weight[...], first[...], second[...], reduce_grad[...] * factor, matrix_rate, matrix_decay)
            for out, value in zip(results, new):
                out[...] = value
        else:
            for lo, hi, at in places[p]:
                own = slice(at, at + hi - lo)
                grad = both[:, lo:hi] * factor
                new = adamw(weight[:, own], first[:, own], second[:, own], grad, matrix_rate, matrix_decay)
                for out, value in zip(results, new):
                    out[:, own] = value
    weight, first, second = states[12:15]
    for out, value in zip(outs[12:15], adamw(weight[...], first[...], second[...], norm_grad * factor, vector_rate, 0.0)):
        out[...] = value
    own = jnp.where(mp_ref[0] == 0, rope[:, :width], rope[:, width:]) * factor
    weight, first, second = states[15:18]
    for h in range(weight.shape[0]):
        grad = own[:, h * HD : h * HD + half]
        for out, value in zip(outs[15:18], adamw(weight[h], first[h], second[h], grad, vector_rate, 0.0)):
            out[h] = value


def optimize(core, states, grads, sums):
    outs = tuple(jax.ShapeDtypeStruct(a.shape, f32) for a in states)
    small = tuple(pltpu.with_memory_space_constraint(a, pltpu.HBM) for a in states[12:])
    args = states[:12] + small + grads + sums
    return pl.pallas_call(
        step_kernel,
        out_shape=(jax.ShapeDtypeStruct((1, 1), f32),) + outs,
        grid_spec=pltpu.PrefetchScalarGridSpec(num_scalar_prefetch=1, grid=()),
        compiler_params=pltpu.CompilerParams(vmem_limit_bytes=16 * MIB),
        name="optimize",
    )(core, *args)


def local(
    size,
    tokens,
    cotangent,
    device_class,
    input_proj,
    output_proj,
    expand_proj,
    reduce_proj,
    norm_params,
    rope_freqs,
    input_first,
    input_second,
    output_first,
    output_second,
    expand_first,
    expand_second,
    reduce_first,
    reduce_second,
    norm_first,
    norm_second,
    rope_first,
    rope_second,
):
    heads = rope_freqs.shape[1]
    width = heads * HD
    pairs = width // LANES
    me = lax.axis_index("dp").astype(jnp.int32)
    rows = input_proj.shape[0]

    hid = expand_proj.shape[1]
    lead = width - LANES
    attn_far = gather_far(input_proj.reshape(rows, 3 * width).astype(bf16), size)
    attn_pieces = gather_near(attn_far, size, 3 * width // 2 // LANES * LANES + LANES)
    expand_shard = jnp.concatenate([expand_proj.astype(bf16), output_proj.astype(bf16)], axis=1)
    expand_far = gather_far(tie(expand_shard, attn_far), size)
    expand_far = tie(expand_far, *attn_pieces[0], *attn_pieces[1])
    expand_pieces = gather_near(expand_far, size, (hid + width) // 2 // LANES * LANES + LANES)
    reduce_far = gather_far(tie(reduce_proj.astype(bf16), expand_far), size)
    reduce_far = tie(reduce_far, *expand_pieces[0], *expand_pieces[1])
    reduce_pieces = gather_near(reduce_far, size, hid // 2)

    column, row_pos, usable = slab_layout(device_class[0])
    gains = norm_params.T
    normed = norm_forward(tokens.astype(f32), norm_params[:, 0], norm_params[:, 1])[0].astype(bf16)
    half = HD // 2
    freqs = jnp.concatenate([rope_freqs, rope_freqs], axis=2).reshape(2, width)
    angles = column[:, None] * freqs[0][None] + row_pos[:, None] * freqs[1][None]
    cosine = jnp.cos(angles)
    sine = jnp.sin(angles) * jnp.where(jnp.arange(width) % HD < half, -1.0, 1.0)[None]
    column = jnp.broadcast_to(column[:, None], (TOK_DEV, LANES))
    row_pos = jnp.broadcast_to(row_pos[:, None], (TOK_DEV, LANES))
    upstream = (cotangent.astype(f32) * usable[:, None]).astype(bf16)

    def product(terms, color, *place):
        return grad_halves(terms, orders(size)[color], size, me, *place)

    attn_whole = whole(attn_pieces, size, me)
    qkv = project(normed, attn_whole, cosine, sine, width)
    mixed, mixed_wide, lse = attend(device_class, qkv, pairs)
    whole_expand = whole(expand_pieces, size, me)
    attn_part = times_columns(mixed, whole_expand, width, hid // width)
    attn_other = traded(attn_part)
    hidden_rows, second_in, activ, slope = widen(tokens, attn_part, attn_other, gains, whole_expand, hid)
    wide = hid // 2
    reduce_halves = [product([(upstream, activ, c, wide)], c) for c in range(2)]
    reduce_last = scatter(reduce_halves, size)
    whole_reduce = whole(reduce_pieces, size, me)
    mlp_part = times_columns(activ, whole_reduce, 2 * wide, 0)
    mlp_other = traded(mlp_part)
    expanded_low, second_part = narrow(upstream, slope, whole_reduce, whole_expand)
    second_other = traded(second_part)
    cuts = (wide + lead, wide + LANES)
    expand_halves = [product([(second_in, expanded_low, c, wide)], c, cuts[c]) for c in range(2)]
    activations, attn_low, mixed_low, sums_two = second_back(
        upstream, second_part, second_other, hidden_rows, mlp_part, mlp_other, gains, whole_expand, width, hid // width
    )
    expand_halves = [
        product([(attn_low, mixed, 0, lead)], 0, cuts[0], wide, expand_halves[0]),
        product([(attn_low, mixed, lead // LANES, LANES)], 1, cuts[1], wide, expand_halves[1]),
    ]
    expand_last = scatter(expand_halves, size)
    back = (device_class, qkv, mixed_low, mixed_wide, lse, cosine, sine, column, row_pos, pairs)
    done = attend_back(*back, 0, pairs - 1)
    dq, dk, dv, turn = attend_back(*back, pairs - 1, pairs, done)
    input_halves = [
        product([(normed, dq, 0, width), (normed, dk, 0, lead)], 0),
        product([(normed, dk, lead // LANES, LANES), (normed, dv, 0, width)], 1),
    ]
    input_keep, input_got, late = scatter(input_halves, size)
    first_part = first_share(dq, dk, dv, attn_whole)
    first_other = traded(first_part)
    input_grad, sums_one = first_back(tokens, first_part, first_other, attn_low, gains)

    turn = tie(turn, sums_one).transpose(1, 0, 2).reshape(2, width)
    turn_other = traded(turn)
    core = lax.axis_index("mp").astype(jnp.int32)
    turns = jnp.where(
        core == 0, jnp.concatenate([turn, turn_other], axis=1), jnp.concatenate([turn_other, turn], axis=1)
    )
    reduce_shard = added(tie(reduce_last[0], late), reduce_last[1])
    both = added(tie(expand_last[0], late), expand_last[1])
    input_shard = added(input_keep, input_got)
    partial_squares = (jnp.sum(both * both) + jnp.sum(reduce_shard * reduce_shard)) + jnp.sum(
        input_shard * input_shard
    )
    squares = partial_squares + lax.ppermute(partial_squares, "mp", [(0, 1), (1, 0)])
    feats = tokens.shape[1]
    vectors = jnp.concatenate([sums_one, sums_two, turns, jnp.zeros((2, feats), f32)], axis=0)
    sums = butterfly(jnp.where(jnp.arange(8)[:, None] == 6, squares, vectors), size)

    def flip(value):
        return value.transpose(1, 0, 2)

    states = (
        tuple(flip(a) for a in (input_proj, input_first, input_second))
        + (output_proj, output_first, output_second)
        + (expand_proj, expand_first, expand_second)
        + (reduce_proj, reduce_first, reduce_second)
        + (norm_params.T, norm_first.T, norm_second.T)
        + tuple(flip(a) for a in (rope_freqs, rope_first, rope_second))
    )
    grads = (input_shard, both, reduce_shard)
    clip_norm, *new = optimize(core[None], states, grads, sums)
    new = (
        [flip(a) for a in new[:3]]
        + new[3:12]
        + [a.T for a in new[12:15]]
        + [flip(a) for a in new[15:]]
    )
    return (activations, input_grad, clip_norm.reshape(()), *new)


def solution(mesh):
    rows, cube, flat, full = P("dp", None), P("dp", None, "mp"), P("dp", "mp"), P()
    rope = P(None, "mp", None)
    in_specs = (
        (rows, rows, P("dp"), cube, flat, flat, flat, full, rope)
        + (cube, cube)
        + (flat,) * 6
        + (full, full, rope, rope)
    )
    out_specs = (rows, rows, full) + (cube,) * 3 + (flat,) * 9 + (full,) * 3 + (rope,) * 3

    def step(*args):
        return local(mesh.shape["dp"], *args)

    step = jax.shard_map(step, mesh=mesh, in_specs=in_specs, out_specs=out_specs, check_vma=False)
    return step
```
